32 devices in a mesh: ctx: 16 (over z, y, x), exp: 2 (over core).
Axes of the slice: x: 2, y: 2, z: 4, core: 2. Of those that a mesh axis runs over, the one named last changes fastest.
Arguments:
- attn_query: bfloat16 [2048, 4096], P('ctx', 'exp'), may hold values from -3 to 3
- attn_key: bfloat16 [2048, 4096], P('ctx', 'exp'), may hold values from -3 to 3
- attn_value: bfloat16 [2048, 4096], P('ctx', 'exp'), may hold values from -6 to 6
- log_decay: float32 [32, 2048], P('exp', 'ctx'), may hold values from -1 to 0
- cotangent: bfloat16 [2048, 4096], P('ctx', 'exp'), may hold values from -6 to 6
- expert_input: bfloat16 [2048, 4096], P('ctx', 'exp'), may hold values from -6 to 6
- router_gates: bfloat16 [2048, 4], P('ctx'), may hold values from 0.049804688 to 0.59765625
- expert_ids: int32 [2048, 4], P('ctx'), may hold values from 0 to 15, all different within a row; in each aligned block of 128 rows (0 to 127, 128 to 255, ...) at most 40 rows name the same one
- up_weights: bfloat16 [16, 4096, 1536], P('ctx', 'exp'), may hold values from -0.09375 to 0.09375
- down_weights: bfloat16 [16, 1536, 4096], P('ctx', None, 'exp'), may hold values from -0.15625 to 0.15625
Outputs:
- query_grad: bfloat16 [2048, 4096], P('ctx', 'exp')
- key_grad: bfloat16 [2048, 4096], P('ctx', 'exp')
- value_grad: bfloat16 [2048, 4096], P('ctx', 'exp')
- input_grad: bfloat16 [2048, 4096], P('ctx', 'exp')
- gate_grad: bfloat16 [2048, 4], P('ctx')
The draws below stay inside these ranges and needn't reach their ends.
Inputs may be any that keep to these rules, and one draw needn't show every extreme that they name: `expert_ids`: each row names 4 different experts. Within the rows of one device (each aligned block of 128 rows) no expert is named more than 40 times, a bound that some block reaches.
All inputs are finite; a program needn't handle non-finite values.
Results may differ from the reference program's by a relative error of at most 0.025.
Values may be sent and summed in bfloat16 or wider, within the bound.
No kernel may reach another device: no remote copies, remote signals or barrier semaphores. Data moves between devices by JAX's collectives and lax.ppermute only.
A program may use at most 128 MiB of HBM per device.

```python
import math
import jax
import jax.numpy as jnp
import numpy as np
from jax import lax

HEAD_TOTAL = 32
HD = 128
HID = 1536
TOP = 4
TOK_DEV = 128
D = 4096
DS = 2048
SEQUENCE_LENGTH = 2048
EXPERTS = 16
CAP = 40
N_CTX = 16
N_EXP = 2


def draw_log_decay(key, part):
    key_rows = jax.random.split(jax.random.fold_in(key, 11), 7)
    slow_share = 0.5
    slow_heads = jax.random.uniform(key_rows[0], (HEAD_TOTAL, 1)) < slow_share
    fast_rate = jax.random.uniform(key_rows[1], (HEAD_TOTAL, 1), minval=1.0 / 50.0, maxval=1.0 / 30.0)
    slow_rate = jax.random.uniform(key_rows[2], (HEAD_TOTAL, 1), minval=0.05, maxval=0.3) / SEQUENCE_LENGTH
    baseline_decay_rate = jnp.where(slow_heads, slow_rate, fast_rate)
    block_multiplier = jnp.exp(jax.random.uniform(key_rows[3], (HEAD_TOTAL, SEQUENCE_LENGTH // TOK_DEV), minval=-0.69, maxval=0.69))
    block_multiplier = jnp.repeat(block_multiplier, TOK_DEV, axis=1)
    jitter_level = jax.random.uniform(key_rows[4], (HEAD_TOTAL, SEQUENCE_LENGTH), minval=0.5, maxval=1.5)
    positions = jax.random.randint(key_rows[5], (HEAD_TOTAL, 2), 0, SEQUENCE_LENGTH)
    selected_flag = jnp.any(jnp.arange(SEQUENCE_LENGTH)[None, :, None] == positions[:, None, :], axis=2)
    spike_magnitude = jax.random.uniform(key_rows[6], (HEAD_TOTAL, SEQUENCE_LENGTH), minval=0.22, maxval=0.69)
    value_rows = baseline_decay_rate * block_multiplier * jitter_level + jnp.where(selected_flag, spike_magnitude, 0.0)
    return (-value_rows).astype(jnp.float32)


def block_scale(rng, extent, cuts, smallest, top_value):
    def one(axis_at, shards_of):
        steps = jax.random.uniform(jax.random.fold_in(jax.random.fold_in(rng, 6), axis_at), (shards_of,), jnp.float32, smallest / len(cuts), top_value / len(cuts))
        return jnp.repeat(jnp.exp(steps), extent[axis_at] // shards_of).reshape((-1,) + (1,) * (len(extent) - axis_at - 1))

    gain = one(*cuts[0])
    for cut in cuts[1:]:
        gain = gain * one(*cut)
    return gain


def deal_out(own_key, own, number, rows, count, top, limit, slope):
    order = jax.random.permutation(own_key, count)
    heavy_load, common = portions_of(count, rows * top, limit, slope, True), portions_of(count, rows * top, limit, slope, False)
    places = jnp.arange(count)

    def named(tallies, turn):
        used = int((tallies > 0).sum())
        fixed = max(1, used // 4)
        shifted = fixed + (places - fixed + turn * (used - fixed)) % max(1, count - fixed)
        return jnp.zeros((count,), jnp.int32).at[order[jnp.where(places < fixed, places, shifted)]].set(jnp.asarray(tallies, jnp.int32))

    tallies = jnp.where(number % 4 == 0, named(heavy_load, number // 4), named(common, number - number // 4 - 1))
    mixed = jax.random.permutation(jax.random.fold_in(own, 3), count)
    donor, sink = mixed[0:count // 2 * 2:2], mixed[1:count // 2 * 2:2]
    room = jnp.minimum(tallies[donor] - 1, limit - tallies[sink]) // 2
    room = jnp.where((donor == order[0]) | (sink == order[0]) | (tallies[sink] == 0), 0, jnp.maximum(room, 0))
    shifted = jax.random.randint(jax.random.fold_in(own, 4), (count // 2,), 0, 1 << 20) % (room + 1)
    tallies = tallies.at[donor].add(-shifted).at[sink].add(shifted)
    items = jnp.searchsorted(jnp.cumsum(tallies), jnp.arange(rows * top), side="right").astype(jnp.int32)
    table = items.reshape(top, rows).T
    table = table[jax.random.permutation(jax.random.fold_in(own, 1), rows)]
    turn = jax.random.randint(jax.random.fold_in(own, 2), (rows, 1), 0, top)
    return jnp.take_along_axis(table, (jnp.arange(top)[None, :] + turn) % top, axis=1)


def portions_of(amount, total, limit, skew, full):
    loads = [(1 << 20) // math.isqrt(rank ** skew) + 1 for rank in range(1, amount + 1)]
    largest = limit if full else min(limit, max(-(-total // amount), total * loads[0] // sum(loads)))
    least = 1 if total - largest >= amount - 1 else 0
    counts, surplus = [largest] + [least] * (amount - 1), total - largest - least * (amount - 1)
    while surplus > 0:
        movable = [i for i in range(1, amount) if counts[i] < largest] or [i for i in range(1, amount) if counts[i] < limit]
        pool, budget = sum([loads[i] for i in movable]), surplus
        for i in movable:
            extra = min(limit - counts[i], max(1, budget * loads[i] // pool), surplus)
            counts[i] = counts[i] + extra
            surplus = surplus - extra
    return np.array(counts)


def gaussian(key, shape, deviation, bound, pieces=(), held_as=jnp.bfloat16):
    drawn = deviation * jax.random.normal(key, shape, jnp.float32)
    if pieces:
        drawn = drawn * block_scale(key, shape, pieces, -0.22, 0.18)
    return jnp.clip(drawn, -bound, bound).astype(held_as)


def setup_inputs(seed: int = 0) -> dict:
    streams_of = jax.random.split(jax.random.key(seed), 11)
    attn_query = gaussian(streams_of[0], (SEQUENCE_LENGTH, D), 0.5, 3.0, ((0, 16), (1, 2)))
    attn_key = gaussian(streams_of[1], (SEQUENCE_LENGTH, D), 0.5, 3.0, ((0, 16), (1, 2)))
    attn_value = gaussian(streams_of[2], (SEQUENCE_LENGTH, D), 1.0, 6.0, ((0, 16), (1, 2)))
    log_decay = draw_log_decay(jax.random.fold_in(streams_of[10], 71), 0)
    cotangent = gaussian(streams_of[4], (SEQUENCE_LENGTH, D), 1.0, 6.0, ((0, 16), (1, 2)))
    expert_input = gaussian(streams_of[5], (SEQUENCE_LENGTH, D), 1.0, 6.0, ((0, 16), (1, 2)))
    router_gates = jnp.clip(0.049804688 + 0.54785156 * jax.random.uniform(streams_of[6], (SEQUENCE_LENGTH, TOP), jnp.float32) ** block_scale(streams_of[6], (SEQUENCE_LENGTH, TOP), ((0, 16),), -0.2, 0.2), 0.049804688, 0.59765625).astype(jnp.bfloat16)
    expert_ids_keys = jax.random.split(jax.random.fold_in(streams_of[7], 1), SEQUENCE_LENGTH // TOK_DEV)
    expert_ids_turns = jax.random.permutation(jax.random.fold_in(streams_of[7], 3), SEQUENCE_LENGTH // TOK_DEV)
    expert_ids = jax.vmap(lambda own, number: deal_out(jax.random.fold_in(streams_of[7], 2), own, number, TOK_DEV, EXPERTS, TOP, CAP, 1))(expert_ids_keys, expert_ids_turns).reshape((SEQUENCE_LENGTH, TOP))
    up_weights = gaussian(streams_of[8], (EXPERTS, D, HID), D ** -0.5, 0.09375, ((0, 16), (1, 2)))
    down_weights = gaussian(streams_of[9], (EXPERTS, HID, D), HID ** -0.5, 0.15625, ((0, 16), (2, 2)))
    return dict(attn_query=attn_query, attn_key=attn_key, attn_value=attn_value, log_decay=log_decay, cotangent=cotangent, expert_input=expert_input, router_gates=router_gates, expert_ids=expert_ids, up_weights=up_weights, down_weights=down_weights)


def rounded(value_rows):
    return lax.optimization_barrier(value_rows.astype(jnp.bfloat16)).astype(jnp.float32)


def silu_slope(pre_act):
    sigmoid_val = jax.nn.sigmoid(pre_act)
    return sigmoid_val * (1.0 + pre_act * (1.0 - sigmoid_val))


def chain_step(running, block_item):
    block_gain, block_term = block_item
    return jnp.exp(block_gain)[:, None, None] * running + block_term, running


def attention_reference(attn_query, attn_key, attn_value, log_decay, cotangent):
    head_shape = (N_CTX, TOK_DEV, HEAD_TOTAL, HD)
    query_all = attn_query.reshape(head_shape).astype(jnp.float32)
    key_all = attn_key.reshape(head_shape).astype(jnp.float32)
    value_all = attn_value.reshape(head_shape).astype(jnp.float32)
    cot_all = cotangent.reshape(head_shape).astype(jnp.float32)
    decay_all = jnp.transpose(log_decay.reshape(HEAD_TOTAL, N_CTX, TOK_DEV), (1, 0, 2))
    cumul = jnp.cumsum(decay_all, axis=2)
    block_total = cumul[:, :, -1]
    head_gain = jnp.transpose(jnp.exp(cumul), (0, 2, 1))[..., None]
    tail_gain = jnp.transpose(jnp.exp(block_total[:, :, None] - cumul), (0, 2, 1))[..., None]
    scaled_key_rows = rounded(tail_gain * key_all)
    scaled_query_rows = rounded(head_gain * query_all)
    local_state = jnp.einsum("nshk,nshv->nhkv", scaled_key_rows, value_all)
    local_adjoint = jnp.einsum("nthk,nthv->nhkv", scaled_query_rows, cot_all)
    zero_state = jnp.zeros((HEAD_TOTAL, HD, HD), jnp.float32)
    _, states = lax.scan(chain_step, zero_state, (block_total, local_state))
    _, adjoints = lax.scan(chain_step, zero_state, (block_total, local_adjoint), reverse=True)
    states = rounded(states)
    adjoints = rounded(adjoints)
    row_index = lax.broadcasted_iota(jnp.int32, (TOK_DEV, TOK_DEV), 0)
    col_index = lax.broadcasted_iota(jnp.int32, (TOK_DEV, TOK_DEV), 1)
    causal = (row_index >= col_index)[None, None, :, :]
    spread = cumul[:, :, :, None] - cumul[:, :, None, :]
    decay_mask = jnp.where(causal, jnp.exp(jnp.where(causal, spread, 0.0)), 0.0)
    cross_terms = jnp.einsum("nthv,nshv->nhts", cot_all, value_all)
    scores = jnp.einsum("nthk,nshk->nhts", query_all, key_all)
    cross_weights = rounded(cross_terms * decay_mask)
    score_weights = rounded(scores * decay_mask)
    query_part = jnp.einsum("nhts,nshk->nthk", cross_weights, key_all)
    query_part = query_part + head_gain * jnp.einsum("nthv,nhkv->nthk", cot_all, states)
    key_part = jnp.einsum("nhts,nthk->nshk", cross_weights, query_all)
    key_part = key_part + tail_gain * jnp.einsum("nshv,nhkv->nshk", value_all, adjoints)
    value_part = jnp.einsum("nhts,nthv->nshv", score_weights, cot_all)
    value_part = value_part + tail_gain * jnp.einsum("nshk,nhkv->nshv", key_all, adjoints)
    scale = 1.0 / HD
    query_grad = (query_part * scale).reshape(SEQUENCE_LENGTH, D).astype(jnp.bfloat16)
    key_grad = (key_part * scale).reshape(SEQUENCE_LENGTH, D).astype(jnp.bfloat16)
    value_grad = (value_part * scale).reshape(SEQUENCE_LENGTH, D).astype(jnp.bfloat16)
    return query_grad, key_grad, value_grad


def slots_of(ids_block):
    flat_ids = ids_block.reshape(-1)
    onehot = (flat_ids[:, None] == jnp.arange(EXPERTS, dtype=jnp.int32)[None, :]).astype(jnp.int32)
    before = jnp.cumsum(onehot, axis=0) - onehot
    return jnp.sum(before * onehot, axis=1).astype(jnp.int32).reshape(ids_block.shape)


def expert_reference(expert_item):
    rows_in, rows_cot, gate_rows, up_one, down_one = expert_item
    row_count = N_CTX * CAP
    split_in = rows_in.reshape(row_count, N_EXP, DS).astype(jnp.float32)
    split_cot = rows_cot.reshape(row_count, N_EXP, DS).astype(jnp.float32)
    split_up = up_one.reshape(N_EXP, DS, HID).astype(jnp.float32)
    split_down = down_one.reshape(HID, N_EXP, DS).astype(jnp.float32)
    pre_act = jnp.sum(rounded(jnp.einsum("rnd,ndh->rnh", split_in, split_up)), axis=1)
    back_rows = jnp.sum(rounded(jnp.einsum("rnd,hnd->rnh", split_cot, split_down)), axis=1)
    gate_back = jnp.sum(back_rows * jax.nn.silu(pre_act), axis=1).astype(jnp.bfloat16)
    gate_col = gate_rows.reshape(row_count).astype(jnp.float32)
    slope_rows = rounded(gate_col[:, None] * back_rows * silu_slope(pre_act))
    rows_grad = jnp.einsum("rh,dh->rd", slope_rows, up_one.astype(jnp.float32)).astype(jnp.bfloat16)
    return rows_grad.reshape(N_CTX, CAP, D), gate_back.reshape(N_CTX, CAP)


def expert_branch(cotangent, expert_input, router_gates, expert_ids, up_weights, down_weights):
    ids_all = expert_ids.reshape(N_CTX, TOK_DEV, TOP).astype(jnp.int32)
    slot_all = jax.vmap(slots_of)(ids_all)
    block_index = lax.broadcasted_iota(jnp.int32, (N_CTX, TOK_DEV, TOP), 0)
    full_shape = (N_CTX, TOK_DEV, TOP, D)
    input_rows = jnp.broadcast_to(expert_input.reshape(N_CTX, TOK_DEV, 1, D), full_shape)
    cot_rows = jnp.broadcast_to(cotangent.reshape(N_CTX, TOK_DEV, 1, D), full_shape)
    buffer_in = jnp.zeros((EXPERTS, N_CTX, CAP, D), jnp.bfloat16).at[ids_all, block_index, slot_all].set(input_rows)
    buffer_cot = jnp.zeros((EXPERTS, N_CTX, CAP, D), jnp.bfloat16).at[ids_all, block_index, slot_all].set(cot_rows)
    buffer_gate = jnp.zeros((EXPERTS, N_CTX, CAP), jnp.bfloat16).at[ids_all, block_index, slot_all].set(
        router_gates.reshape(N_CTX, TOK_DEV, TOP))
    grad_buffer, gate_buffer = lax.map(expert_reference, (buffer_in, buffer_cot, buffer_gate, up_weights, down_weights))
    picked = grad_buffer[ids_all, block_index, slot_all].astype(jnp.float32)
    input_grad = jnp.sum(picked, axis=2).reshape(SEQUENCE_LENGTH, D).astype(jnp.bfloat16)
    gate_grad = gate_buffer[ids_all, block_index, slot_all].reshape(SEQUENCE_LENGTH, TOP)
    return input_grad, gate_grad


def reference(attn_query, attn_key, attn_value, log_decay, cotangent, expert_input, router_gates, expert_ids, up_weights, down_weights):
    query_grad, key_grad, value_grad = attention_reference(attn_query, attn_key, attn_value, log_decay, cotangent)
    input_grad, gate_grad = expert_branch(cotangent, expert_input, router_gates, expert_ids, up_weights, down_weights)
    return (query_grad, key_grad, value_grad, input_grad, gate_grad)
```

```python
import jax
import jax.numpy as jnp
from jax import lax
from jax.experimental import pallas as pl
from jax.experimental.pallas import tpu as pltpu
from jax.sharding import PartitionSpec as P

INNER = 4
META = 128
PAD = 16
F32 = jnp.float32
BF16 = jnp.bfloat16


def flip(x, m):
    n = lax.axis_size("ctx")
    return lax.ppermute(x, "ctx", [(i, i ^ m) for i in range(n)])


def ring(x):
    n = lax.axis_size("ctx")
    return lax.ppermute(x, "ctx", [(i, (i + INNER) % n) for i in range(n)])


def upward(x):
    n = lax.axis_size("ctx")
    return lax.ppermute(x, "ctx", [(i, i + INNER) for i in range(n - INNER)])


def downward(x):
    n = lax.axis_size("ctx")
    return lax.ppermute(x, "ctx", [(i + INNER, i) for i in range(n - INNER)])


def across(x):
    if lax.axis_size("exp") == 2:
        other = lax.ppermute(x, "exp", [(0, 1), (1, 0)])
        return x.astype(F32) + other.astype(F32)
    return lax.psum(x, "exp").astype(F32)


def silu_slope(pre_act):
    sig = jax.nn.sigmoid(pre_act)
    return sig * (1.0 + pre_act * (1.0 - sig))


def dot(a, b, ca, cb):
    return lax.dot_general(a, b, (((ca,), (cb,)), ((), ())), preferred_element_type=F32)


def split_rows(gain):
    high = gain.astype(BF16).astype(F32)
    mid = (gain - high).astype(BF16).astype(F32)
    low = gain - high - mid
    row = lax.broadcasted_iota(jnp.int32, (PAD, gain.shape[1]), 0)
    out = jnp.where(row == 0, high, jnp.where(row == 1, mid, jnp.where(row == 2, low, 0.0)))
    return out.astype(BF16)


def join_rows(rows):
    rows = rows.astype(F32)
    return rows[0:1] + rows[1:2] + rows[2:3]


def local_kernel(q_ref, k_ref, v_ref, c_ref, b_ref, out_ref):
    heads, length = b_ref.shape
    size = q_ref.shape[1] // heads
    for h in range(heads):
        cols = slice(h * size, (h + 1) * size)
        decay = jnp.broadcast_to(b_ref[h : h + 1, :], (length, length)).T
        total = decay[length - 1 : length, :]
        scaled_k = (jnp.exp(total - decay) * k_ref[:, cols].astype(F32)).astype(BF16)
        scaled_q = (jnp.exp(decay) * q_ref[:, cols].astype(F32)).astype(BF16)
        out_ref[h, 0:size, :] = dot(scaled_k, v_ref[:, cols], 0, 0).astype(BF16)
        out_ref[h, size : 2 * size, :] = dot(scaled_q, c_ref[:, cols], 0, 0).astype(BF16)
        out_ref[h, 2 * size :, :] = split_rows(jnp.exp(total))


def plane_kernel(p_ref, x0, x1, x2, x3, up_ref, down_ref):
    place = p_ref[0]
    spots = [place ^ m for m in range(INNER)]
    xs = (x0, x1, x2, x3)
    size = x0.shape[2]
    for h in range(x0.shape[0]):
        gains = [join_rows(x[h, 2 * size :, :]) for x in xs]
        ones = jnp.ones_like(gains[0])
        up = jnp.zeros((size, size), F32)
        down = jnp.zeros((size, size), F32)
        for m in range(INNER):
            after, before = ones, ones
            for j in range(INNER):
                after = after * jnp.where(spots[j] > spots[m], gains[j], ones)
                before = before * jnp.where(spots[j] < spots[m], gains[j], ones)
            up = up + after * xs[m][h, 0:size, :].astype(F32)
            down = down + before * xs[m][h, size : 2 * size, :].astype(F32)
        rows = split_rows(gains[0] * gains[1] * gains[2] * gains[3])
        up_ref[h, 0:size, :] = up.astype(BF16)
        up_ref[h, size:, :] = rows
        down_ref[h, 0:size, :] = down.astype(BF16)
        down_ref[h, size:, :] = rows


def spread_kernel(count, p_ref, *refs):
    place = p_ref[0]
    spots = [place ^ m for m in range(INNER)]
    xs, ups, downs = refs[:INNER], refs[INNER : INNER + count], refs[INNER + count : INNER + 2 * count]
    outs = refs[INNER + 2 * count :]
    heads, _, size = xs[0].shape
    for h in range(heads):
        gains = [join_rows(x[h, 2 * size :, :]) for x in xs]
        ones = jnp.ones_like(gains[0])
        zeros = jnp.zeros_like(gains[0])
        carried = []
        for chain in (ups, downs):
            weight = ones
            total = jnp.zeros((size, size), F32)
            for ref in chain:
                total = total + weight * ref[h, 0:size, :].astype(F32)
                weight = weight * join_rows(ref[h, size:, :])
            carried.append(total)
        keys = [x[h, 0:size, :].astype(F32) for x in xs]
        queries = [x[h, size : 2 * size, :].astype(F32) for x in xs]
        for m in range(INNER):
            first, last = ones, ones
            for j in range(INNER):
                first = first * jnp.where(spots[j] < spots[m], gains[j], ones)
                last = last * jnp.where(spots[j] > spots[m], gains[j], ones)
            state = first * carried[0]
            adjoint = last * carried[1]
            for i in range(INNER):
                if i == m:
                    continue
                between = ones
                for j in range(INNER):
                    if j == m or j == i:
                        continue
                    inside = ((spots[j] > spots[i]) & (spots[j] < spots[m])) | (
                        (spots[j] < spots[i]) & (spots[j] > spots[m])
                    )
                    between = between * jnp.where(inside, gains[j], ones)
                state = state + jnp.where(spots[i] < spots[m], between, zeros) * keys[i]
                adjoint = adjoint + jnp.where(spots[i] > spots[m], between, zeros) * queries[i]
            outs[m][h, 0:size, :] = state.astype(BF16)
            outs[m][h, size:, :] = adjoint.astype(BF16)


def grads_kernel(p_ref, q_ref, k_ref, v_ref, c_ref, b_ref, s0, s1, s2, s3, dq_ref, dk_ref, dv_ref):
    place = p_ref[0]
    states = (s0, s1, s2, s3)
    share, _, size = s0.shape
    length = q_ref.shape[0]
    row = lax.broadcasted_iota(jnp.int32, (length, length), 0)
    col = lax.broadcasted_iota(jnp.int32, (length, length), 1)
    causal = row >= col
    scale = 1.0 / size
    for m in range(INNER):
        quarter = place ^ m
        for i in range(share):
            head = quarter * share + i
            cols = pl.ds(pl.multiple_of(head * size, size), size)
            across_rows = jnp.broadcast_to(b_ref[pl.ds(head, 1), :], (length, length))
            decay = across_rows.T
            total = decay[length - 1 : length, :]
            mask = jnp.where(causal, jnp.exp(jnp.where(causal, decay - across_rows, 0.0)), 0.0)
            lead = jnp.exp(decay)
            tail = jnp.exp(total - decay)
            q, k, v, c = q_ref[:, cols], k_ref[:, cols], v_ref[:, cols], c_ref[:, cols]
            state = states[m][i, 0:size, :]
            adjoint = states[m][i, size : 2 * size, :]
            w = (dot(c, v, 1, 1) * mask).astype(BF16)
            z = (dot(q, k, 1, 1) * mask).astype(BF16)
            dq = dot(w, k, 1, 0) + lead * dot(c, state, 1, 1)
            dk = dot(w, q, 0, 0) + tail * dot(v, adjoint, 1, 1)
            dv = dot(z, c, 0, 0) + tail * dot(k, adjoint, 1, 0)
            dq_ref[:, cols] = (dq * scale).astype(BF16)
            dk_ref[:, cols] = (dk * scale).astype(BF16)
            dv_ref[:, cols] = (dv * scale).astype(BF16)


PARAMS = pltpu.CompilerParams(vmem_limit_bytes=40 * 1024 * 1024)
SCALAR = pl.BlockSpec(memory_space=pltpu.SMEM)


def vmem(count):
    return [pl.BlockSpec(memory_space=pltpu.VMEM) for _ in range(count)]


def attention_local(q, k, v, c, cumul):
    heads = cumul.shape[0]
    size = q.shape[1] // heads
    return pl.pallas_call(
        local_kernel,
        out_shape=jax.ShapeDtypeStruct((heads, 2 * size + PAD, size), BF16),
        in_specs=vmem(5),
        out_specs=vmem(1)[0],
        compiler_params=PARAMS,
        name="local_states",
    )(q, k, v, c, cumul)


def plane_sums(place, xs):
    share, _, size = xs[0].shape
    shape = jax.ShapeDtypeStruct((share, size + PAD, size), BF16)
    return pl.pallas_call(
        plane_kernel,
        out_shape=(shape, shape),
        in_specs=[SCALAR] + vmem(INNER),
        out_specs=tuple(vmem(2)),
        compiler_params=PARAMS,
        name="plane_sums",
    )(place, *xs)


def spread_states(place, xs, ups, downs):
    share, _, size = xs[0].shape
    count = len(ups)
    shape = jax.ShapeDtypeStruct((share, 2 * size, size), BF16)

    def kernel(*refs):
        spread_kernel(count, *refs)

    return pl.pallas_call(
        kernel,
        out_shape=(shape,) * INNER,
        in_specs=[SCALAR] + vmem(INNER + 2 * count),
        out_specs=tuple(vmem(INNER)),
        compiler_params=PARAMS,
        name="spread_states",
    )(place, *xs, *ups, *downs)


def attention_grads(place, q, k, v, c, cumul, states):
    shape = jax.ShapeDtypeStruct(q.shape, BF16)
    return pl.pallas_call(
        grads_kernel,
        out_shape=(shape,) * 3,
        in_specs=[SCALAR] + vmem(5 + INNER),
        out_specs=tuple(vmem(3)),
        compiler_params=PARAMS,
        name="attention_grads",
    )(place, q, k, v, c, cumul, *states)


def placement(meta, experts_at, slots_at, top):
    tokens = meta.shape[0]
    ids = meta[:, :top].astype(F32)
    gates = meta[:, top : 2 * top].astype(F32)
    named = jnp.zeros((tokens, experts_at.shape[1]), F32)
    weight = named
    for j in range(top):
        same = (ids[:, j : j + 1] == experts_at).astype(F32)
        named = named + same
        weight = weight + same * gates[:, j : j + 1]
    row = lax.broadcasted_iota(jnp.int32, (tokens, tokens), 0)
    col = lax.broadcasted_iota(jnp.int32, (tokens, tokens), 1)
    rank = dot((row > col).astype(BF16), named.astype(BF16), 1, 0)
    here = (named > 0.0) & (rank == slots_at)
    return here.astype(BF16), jnp.where(here, weight, 0.0).astype(BF16)


def body(q, k, v, log_decay, cot, expert_input, router_gates, expert_ids, up_weights, down_weights):
    n = lax.axis_size("ctx")
    planes = n // INNER
    index = lax.axis_index("ctx")
    place = (index % INNER).astype(jnp.int32)
    plane = index // INNER
    tokens, width = expert_input.shape
    top = expert_ids.shape[1]
    cap = 5 * tokens * top // (4 * n)
    up, down = up_weights[0], down_weights[0]

    meta = jnp.concatenate(
        [expert_ids.astype(BF16), router_gates, jnp.zeros((tokens, META - 2 * top), BF16)], axis=1
    )
    blocks = [jnp.concatenate([expert_input, cot, meta], axis=1)]
    for _ in range(planes - 1):
        blocks.append(ring(blocks[-1]))

    length = q.shape[0]
    row = lax.broadcasted_iota(jnp.int32, (length, length), 0)
    col = lax.broadcasted_iota(jnp.int32, (length, length), 1)
    cumul = jnp.dot(log_decay, (row <= col).astype(F32), precision=lax.Precision.HIGHEST)
    local = attention_local(q, k, v, cot, cumul)
    heads = local.shape[0]
    quarters = local.reshape((INNER, heads // INNER) + local.shape[1:])
    spot = place.reshape(1)
    xs = [lax.dynamic_index_in_dim(quarters, place ^ m, 0, False) for m in range(INNER)]
    xs = [xs[0]] + [flip(xs[m], m) for m in range(1, INNER)]
    rising, falling = plane_sums(spot, xs)
    ups, downs = [], []
    for _ in range(planes - 1):
        rising, falling = upward(rising), downward(falling)
        ups.append(rising)
        downs.append(falling)
    states = spread_states(spot, xs, ups, downs)
    states = [states[0]] + [flip(states[m], m) for m in range(1, INNER)]
    query_grad, key_grad, value_grad = attention_grads(spot, q, k, v, cot, cumul, states)

    j = lax.broadcasted_iota(jnp.int32, (1, INNER * cap), 1)
    experts_at = (plane * INNER + (place ^ (j // cap))).astype(F32)
    slots_at = (j % cap).astype(F32)
    mine = lax.broadcasted_iota(jnp.int32, (1, META), 1) == index
    carried = None
    partials = {}

    def serve(block):
        here, weight = placement(block[:, 2 * width :], experts_at, slots_at, top)
        rows = dot(here, block[:, : 2 * width], 0, 0).astype(BF16)
        parts = [rows[m * cap : (m + 1) * cap] for m in range(INNER)]
        parts = [parts[0]] + [flip(parts[m], m) for m in range(1, INNER)]
        rows = jnp.concatenate(parts, axis=0)
        pre = across(dot(rows[:, :width], up, 1, 0).astype(BF16))
        back = across(dot(rows[:, width:], down, 1, 1).astype(BF16))
        sig = jax.nn.sigmoid(pre)
        gate_back = jnp.sum(back * pre * sig, axis=1, keepdims=True)
        slope = (back * (sig * (1.0 + pre * (1.0 - sig)))).astype(BF16)
        grads = dot(slope, up, 1, 1).astype(BF16)
        gate_rows = jnp.where(mine, gate_back, 0.0).astype(BF16)
        grads = jnp.concatenate([grads, gate_rows], axis=1)
        parts = [grads[m * cap : (m + 1) * cap] for m in range(INNER)]
        parts = [parts[0]] + [flip(parts[m], m) for m in range(1, INNER)]
        grads = jnp.concatenate(parts, axis=0)
        return dot(weight, grads[:, :width], 1, 0), dot(here, grads[:, width:], 1, 0)

    for r in range(planes):
        partials[r] = serve(blocks[r])
    carried = None
    for r in list(range(1, planes)) + [0]:
        total = jnp.concatenate(partials[r], axis=1)
        if carried is not None:
            total = total + ring(carried).astype(F32)
        carried = total.astype(BF16)
    input_grad = carried[:, :width]
    by_expert = carried[:, width:].astype(F32)
    lane = lax.broadcasted_iota(jnp.int32, (1, META), 1)
    gate_grad = jnp.concatenate(
        [
            jnp.sum(jnp.where(expert_ids[:, j : j + 1] == lane, by_expert, 0.0), axis=1, keepdims=True)
            for j in range(top)
        ],
        axis=1,
    )
    return (query_grad, key_grad, value_grad, input_grad, gate_grad.astype(BF16))


def solution(mesh):
    rows = P("ctx", "exp")
    return jax.shard_map(
        body,
        mesh=mesh,
        in_specs=(
            rows,
            rows,
            rows,
            P("exp", "ctx"),
            rows,
            rows,
            P("ctx", None),
            P("ctx", None),
            P("ctx", "exp", None),
            P("ctx", None, "exp"),
        ),
        out_specs=(rows, rows, rows, rows, P("ctx", None)),
        check_vma=False,
    )
```

```python
import jax
import jax.numpy as jnp
from jax import lax
from jax.experimental import pallas as pl
from jax.experimental.pallas import tpu as pltpu
from jax.sharding import PartitionSpec as P

INNER = 4
META = 128
PAD = 8
STATE_ROWS = 40
F32 = jnp.float32
BF16 = jnp.bfloat16


def flip(x, m):
    n = lax.axis_size("ctx")
    return lax.ppermute(x, "ctx", [(i, i ^ m) for i in range(n)])


def exchange(parts):
    return [parts[0]] + [flip(parts[m], m) for m in range(1, INNER)]


def ring(x):
    n = lax.axis_size("ctx")
    return lax.ppermute(x, "ctx", [(i, (i + INNER) % n) for i in range(n)])


def plane_flip(x, d):
    n = lax.axis_size("ctx")
    return lax.ppermute(x, "ctx", [(i, i ^ (INNER * d)) for i in range(n)])


def dot(a, b, ca, cb):
    return lax.dot_general(a, b, (((ca,), (cb,)), ((), ())), preferred_element_type=F32)


PARAMS = pltpu.CompilerParams(vmem_limit_bytes=28 * 1024 * 1024)
IN_SMEM = pl.BlockSpec(memory_space=pltpu.SMEM)
IN_VMEM = pl.BlockSpec(memory_space=pltpu.VMEM)
ANYWHERE = pl.BlockSpec(memory_space=pl.ANY)
IN_HBM = pl.BlockSpec(memory_space=pltpu.HBM)


def call(kernel, name, outs, specs, *args, scratch=(), needs=(), where=IN_VMEM):
    shapes = [jax.ShapeDtypeStruct(shape, dtype) for shape, dtype in outs]
    count, skip = len(args), len(needs)

    def run(*refs):
        kernel(*refs[:count], *refs[count + skip :])

    return pl.pallas_call(
        run,
        out_shape=shapes,
        in_specs=list(specs) + [ANYWHERE] * skip,
        out_specs=[where] * len(shapes),
        scratch_shapes=list(scratch),
        compiler_params=PARAMS,
        name=name,
    )(*args, *needs)


def split_rows(gain):
    high = gain.astype(BF16).astype(F32)
    mid = (gain - high).astype(BF16).astype(F32)
    low = gain - high - mid
    row = lax.broadcasted_iota(jnp.int32, (PAD, gain.shape[1]), 0)
    out = jnp.where(row == 0, high, jnp.where(row == 1, mid, jnp.where(row == 2, low, 0.0)))
    return out.astype(BF16)


def join_rows(rows):
    rows = rows.astype(F32)
    return rows[0:1] + rows[1:2] + rows[2:3]


def states_into(place, q_ref, k_ref, v_ref, c_ref, b_ref, outs):
    heads, length = b_ref.shape
    width = q_ref.shape[1]
    size = width // heads
    share = heads // INNER
    chunk = size // 4
    for m in range(INNER):
        for i in range(share):
            head = (place ^ m) * share + i
            cols = pl.ds(pl.multiple_of(head * size, size), size)
            decay = jnp.broadcast_to(b_ref[pl.ds(head, 1), :], (length, length)).T
            total = decay[length - 1 : length, :]
            scaled_k = (jnp.exp(total - decay) * k_ref[:, cols].astype(F32)).astype(BF16)
            scaled_q = (jnp.exp(decay) * q_ref[:, cols].astype(F32)).astype(BF16)
            state = dot(scaled_k, v_ref[:, cols], 0, 0).astype(BF16)
            adjoint = dot(scaled_q, c_ref[:, cols], 0, 0).astype(BF16)
            gains = split_rows(jnp.exp(total))
            for part in range(4):
                rows = slice(part * chunk, (part + 1) * chunk)
                left = slice((4 * i + part) * size, (4 * i + part + 1) * size)
                right = slice(width + (4 * i + part) * size, width + (4 * i + part + 1) * size)
                outs[m][0:chunk, left] = state[rows]
                outs[m][0:chunk, right] = adjoint[rows]
                outs[m][chunk:STATE_ROWS, left] = gains
                outs[m][chunk:STATE_ROWS, right] = gains


def plane_kernel(p_ref, x0, x1, x2, x3, out_ref):
    spots = [p_ref[0] ^ m for m in range(INNER)]
    xs = (x0, x1, x2, x3)
    width = out_ref.shape[1] // 2
    rows = STATE_ROWS - PAD
    gains = [join_rows(x[rows:STATE_ROWS, 0:width]) for x in xs]
    ones = jnp.ones_like(gains[0])
    up = jnp.zeros((rows, width), F32)
    down = jnp.zeros((rows, width), F32)
    for m in range(INNER):
        behind, before = ones, ones
        for j in range(INNER):
            behind = behind * jnp.where(spots[j] > spots[m], gains[j], ones)
            before = before * jnp.where(spots[j] < spots[m], gains[j], ones)
        up = up + behind * xs[m][0:rows, 0:width].astype(F32)
        down = down + before * xs[m][0:rows, width:].astype(F32)
    total = split_rows(gains[0] * gains[1] * gains[2] * gains[3])
    out_ref[0:rows, 0:width] = up.astype(BF16)
    out_ref[0:rows, width:] = down.astype(BF16)
    out_ref[rows:, 0:width] = total
    out_ref[rows:, width:] = total


def scan_planes(plane, own, others):
    width = own.shape[1] // 2
    rows = STATE_ROWS - PAD
    gain = join_rows(own[rows:, 0:width])
    ones = jnp.ones_like(gain)
    up = own[0:rows, 0:width].astype(F32)
    down = own[0:rows, width:].astype(F32)
    below = jnp.zeros_like(up)
    above = jnp.zeros_like(down)
    gain_below, gain_above = ones, ones
    for number, ref in enumerate(others):
        high = (plane & (1 << number)) != 0
        their_up = ref[0:rows, 0:width].astype(F32)
        their_down = ref[0:rows, width:].astype(F32)
        their_gain = join_rows(ref[rows:, 0:width])
        below = jnp.where(high, below + gain_below * their_up, below)
        gain_below = jnp.where(high, gain_below * their_gain, gain_below)
        above = jnp.where(high, above, above + gain_above * their_down)
        gain_above = jnp.where(high, gain_above, gain_above * their_gain)
        up = jnp.where(high, up + gain * their_up, their_up + their_gain * up)
        down = jnp.where(high, their_down + their_gain * down, down + gain * their_down)
        gain = gain * their_gain
    return up, down, gain, below, gain_below, above, gain_above


def join_kernel(last, p_ref, own, *refs):
    out_ref = refs[-1]
    plane = p_ref[1]
    rows = STATE_ROWS - PAD
    up, down, gain, *_ = scan_planes(plane, own, refs[:-1])
    if last:
        high = (plane & (1 << (len(refs) - 1))) != 0
        out_ref[0:rows, :] = jnp.where(high, down, up).astype(BF16)
        out_ref[rows:, :] = split_rows(gain)
        return
    width = up.shape[1]
    out_ref[0:rows, 0:width] = up.astype(BF16)
    out_ref[0:rows, width:] = down.astype(BF16)
    out_ref[rows:, 0:width] = split_rows(gain)
    out_ref[rows:, width:] = split_rows(gain)


def spread_kernel(p_ref, x0, x1, x2, x3, own, *refs):
    spots = [p_ref[0] ^ m for m in range(INNER)]
    plane = p_ref[1]
    xs, outs = (x0, x1, x2, x3), refs[-INNER:]
    others, final = refs[: -INNER - 1], refs[-INNER - 1]
    width = own.shape[1] // 2
    rows = STATE_ROWS - PAD
    gains = [join_rows(x[rows:STATE_ROWS, 0:width]) for x in xs]
    ones = jnp.ones_like(gains[0])
    zeros = jnp.zeros_like(gains[0])
    _, _, _, below, gain_below, above, gain_above = scan_planes(plane, own, others)
    high = (plane & (1 << len(others))) != 0
    far = final[0:rows, :].astype(F32)
    below = jnp.where(high, below + gain_below * far, below)
    above = jnp.where(high, above, above + gain_above * far)
    keys = [x[0:rows, 0:width].astype(F32) for x in xs]
    queries = [x[0:rows, width:].astype(F32) for x in xs]
    for m in range(INNER):
        first, last = ones, ones
        for j in range(INNER):
            first = first * jnp.where(spots[j] < spots[m], gains[j], ones)
            last = last * jnp.where(spots[j] > spots[m], gains[j], ones)
        state = first * below
        adjoint = last * above
        for i in range(INNER):
            if i == m:
                continue
            between = ones
            for j in range(INNER):
                if j == m or j == i:
                    continue
                inside = ((spots[j] > spots[i]) & (spots[j] < spots[m])) | (
                    (spots[j] < spots[i]) & (spots[j] > spots[m])
                )
                between = between * jnp.where(inside, gains[j], ones)
            state = state + jnp.where(spots[i] < spots[m], between, zeros) * keys[i]
            adjoint = adjoint + jnp.where(spots[i] > spots[m], between, zeros) * queries[i]
        outs[m][0:rows, :] = state.astype(BF16)
        outs[m][rows:, :] = adjoint.astype(BF16)


def grads_kernel(p_ref, q_ref, k_ref, v_ref, c_ref, b_ref, s0, s1, s2, s3, dq_ref, dk_ref, dv_ref):
    place = p_ref[0]
    states = (s0, s1, s2, s3)
    heads, length = b_ref.shape
    size = q_ref.shape[1] // heads
    share = heads // INNER
    chunk = size // 4
    row = lax.broadcasted_iota(jnp.int32, (length, length), 0)
    col = lax.broadcasted_iota(jnp.int32, (length, length), 1)
    causal = row >= col
    scale = 1.0 / size
    for m in range(INNER):
        quarter = place ^ m
        for i in range(share):
            head = quarter * share + i
            cols = pl.ds(pl.multiple_of(head * size, size), size)
            across_rows = jnp.broadcast_to(b_ref[pl.ds(head, 1), :], (length, length))
            decay = across_rows.T
            total = decay[length - 1 : length, :]
            mask = jnp.where(causal, jnp.exp(jnp.where(causal, decay - across_rows, 0.0)), 0.0)
            lead = jnp.exp(decay)
            tail = jnp.exp(total - decay)
            q, k, v, c = q_ref[:, cols], k_ref[:, cols], v_ref[:, cols], c_ref[:, cols]
            tiles = [slice((4 * i + part) * size, (4 * i + part + 1) * size) for part in range(4)]
            state = jnp.concatenate([states[m][0:chunk, t] for t in tiles], axis=0)
            adjoint = jnp.concatenate([states[m][chunk : 2 * chunk, t] for t in tiles], axis=0)
            w = (dot(c, v, 1, 1) * mask).astype(BF16)
            z = (dot(q, k, 1, 1) * mask).astype(BF16)
            dq = dot(w, k, 1, 0) + lead * dot(c, state, 1, 1)
            dk = dot(w, q, 0, 0) + tail * dot(v, adjoint, 1, 1)
            dv = dot(z, c, 0, 0) + tail * dot(k, adjoint, 1, 0)
            dq_ref[:, cols] = (dq * scale).astype(BF16)
            dk_ref[:, cols] = (dk * scale).astype(BF16)
            dv_ref[:, cols] = (dv * scale).astype(BF16)


def pack_kernel(x_hbm, c_hbm, ids_hbm, gates_hbm, out_hbm, ids_ref, gates_ref, meta_ref, sems):
    tokens, width = x_hbm.shape
    top = ids_hbm.shape[0]
    pairs = [
        (ids_hbm, ids_ref),
        (gates_hbm, gates_ref),
        (x_hbm, out_hbm.at[:, 0:width]),
        (c_hbm, out_hbm.at[:, width : 2 * width]),
    ]
    copies = [pltpu.make_async_copy(a, b, sems.at[i]) for i, (a, b) in enumerate(pairs)]
    for copy in copies:
        copy.start()
    copies[0].wait()
    copies[1].wait()
    lists = [ids_ref[...].astype(F32), gates_ref[...].astype(F32)]
    lists.append(jnp.zeros((META - 2 * top, tokens), F32))
    meta_ref[...] = jnp.concatenate(lists, axis=0).T.astype(BF16)
    rest = pltpu.make_async_copy(meta_ref, out_hbm.at[:, 2 * width :], sems.at[4])
    rest.start()
    copies[2].wait()
    copies[3].wait()
    rest.wait()


def dispatch(block_ref, place, plane, cap, top):
    tokens, columns = block_ref.shape
    width = columns - META
    meta = block_ref[:, width:].astype(F32)
    j = lax.broadcasted_iota(jnp.int32, (tokens, INNER * cap), 1)
    part = jnp.zeros_like(j)
    for m in range(1, INNER):
        part = part + (j >= m * cap).astype(jnp.int32)
    expert = plane * INNER + (place ^ part)
    slots = (j - part * cap).astype(F32)
    expert = expert.astype(F32)
    named = jnp.zeros((tokens, INNER * cap), F32)
    weight = named
    for t in range(top):
        same = meta[:, t : t + 1] == expert
        named = jnp.where(same, 1.0, named)
        weight = jnp.where(same, meta[:, top + t : top + t + 1], weight)
    row = lax.broadcasted_iota(jnp.int32, (tokens, tokens), 0)
    col = lax.broadcasted_iota(jnp.int32, (tokens, tokens), 1)
    earlier = jnp.where(row > col, 1.0, 0.0).astype(BF16)
    rank = dot(earlier, named.astype(BF16), 1, 0)
    here = jnp.where(rank == slots, named, 0.0)
    weight = here * weight
    here = here.astype(BF16)
    rows = dot(here, block_ref[:, 0:width], 0, 0).astype(BF16)
    return rows, here, weight.astype(BF16)


def combine_kernel(base, has_carry, last, *refs):
    here_ref, weight_ref = refs[0:2]
    parts = refs[2 : 2 + INNER]
    cap = here_ref.shape[1] // INNER
    width = parts[0].shape[1] - META
    rows = jnp.concatenate([x[base : base + cap, :] for x in parts], axis=0)
    grads = dot(weight_ref[...], rows[:, 0:width], 1, 0)
    gates = dot(here_ref[...], rows[:, width:], 1, 0)
    if has_carry:
        carry = refs[2 + INNER]
        grads = grads + carry[:, 0:width].astype(F32)
        gates = gates + carry[:, width:].astype(F32)
    if not last:
        refs[-1][:, 0:width] = grads.astype(BF16)
        refs[-1][:, width:] = gates.astype(BF16)
        return
    ids_ref, grad_ref, gate_ref = refs[-3:]
    grad_ref[...] = grads.astype(BF16)
    top, tokens = ids_ref.shape
    gates = gates.T
    row = lax.broadcasted_iota(jnp.int32, (META, tokens), 0)
    for t in range(top):
        mine = ids_ref[t : t + 1, :] == row
        picked = jnp.sum(jnp.where(mine, gates, 0.0), axis=0, keepdims=True)
        gate_ref[t : t + 1, :] = picked.astype(BF16)


def front_kernel(cap, *refs):
    parts, (up_ref, down_ref, pre_ref, back_ref) = refs[:-4], refs[-4:]
    width = up_ref.shape[1]
    rows = jnp.concatenate([x[x.shape[0] - cap :, :] for x in parts], axis=0)
    pre_ref[...] = dot(rows[:, 0:width], up_ref[0], 1, 0).astype(BF16)
    back_ref[...] = dot(rows[:, width:], down_ref[0], 1, 1).astype(BF16)


def back_kernel(slots, cap, i_ref, *refs):
    sums, up_ref, outs = refs[: -INNER - 1], refs[-INNER - 1], refs[-INNER:]
    width = up_ref.shape[1]
    half = len(sums) // 2
    pre, back = sums[0][...].astype(F32), sums[half][...].astype(F32)
    if half == 2:
        pre, back = pre + sums[1][...].astype(F32), back + sums[3][...].astype(F32)
    sig = 1.0 / (1.0 + jnp.exp(-pre))
    gate_back = jnp.sum(back * pre * sig, axis=1, keepdims=True)
    slope = (back * (sig * (1.0 + pre * (1.0 - sig)))).astype(BF16)
    lane = lax.broadcasted_iota(jnp.int32, (slope.shape[0], META), 1)
    gates = jnp.where(lane == i_ref[0], gate_back, 0.0).astype(BF16)
    grads = dot(slope, up_ref[0], 1, 1).astype(BF16)
    for s in range(slots):
        for m in range(INNER):
            source = slice((s * INNER + m) * cap, (s * INNER + m + 1) * cap)
            target = slice(s * cap, (s + 1) * cap)
            outs[m][target, 0:width] = grads[source]
            outs[m][target, width:] = gates[source]


def body(q, k, v, log_decay, cot, expert_input, router_gates, expert_ids, up_weights, down_weights):
    n = lax.axis_size("ctx")
    planes = n // INNER
    index = lax.axis_index("ctx").astype(jnp.int32)
    spots = jnp.stack([index % INNER, index // INNER])
    where = index.reshape(1)
    tokens, width = expert_input.shape
    top = expert_ids.shape[1]
    cap = 5 * tokens * top // (4 * n)
    heads = log_decay.shape[0]
    size = width // heads
    hidden = up_weights.shape[2]
    ids, gates = expert_ids.T, router_gates.T

    (block,) = call(
        pack_kernel,
        "pack",
        [((tokens, 2 * width + META), BF16)],
        [IN_HBM] * 4,
        expert_input,
        cot,
        ids,
        gates,
        scratch=[
            pltpu.VMEM((top, tokens), expert_ids.dtype),
            pltpu.VMEM((top, tokens), BF16),
            pltpu.VMEM((tokens, META), BF16),
            pltpu.SemaphoreType.DMA((5,)),
        ],
        where=IN_HBM,
    )
    blocks = [block]
    for _ in range(planes - 1):
        blocks.append(ring(blocks[-1]))

    row = lax.broadcasted_iota(jnp.int32, (tokens, tokens), 0)
    col = lax.broadcasted_iota(jnp.int32, (tokens, tokens), 1)
    cumul = jnp.dot(log_decay, (row <= col).astype(F32), precision=lax.Precision.HIGHEST)
    table = ((tokens, INNER * cap), BF16)
    sent, tables, answers, carry = {}, {}, {}, []

    def dispatch_into(start, p_ref, x_ref, outs):
        rows, here, weight = dispatch(x_ref, p_ref[0], p_ref[1], cap, top)
        for m in range(INNER):
            outs[m][start:, :] = rows[m * cap : (m + 1) * cap]
        outs[INNER][...] = here
        outs[INNER + 1][...] = weight

    def first_kernel(p_ref, x_ref, q_ref, k_ref, v_ref, c_ref, b_ref, *outs):
        states_into(p_ref[0], q_ref, k_ref, v_ref, c_ref, b_ref, outs)
        dispatch_into(STATE_ROWS, p_ref, x_ref, outs)

    def next_kernel(p_ref, x_ref, *outs):
        dispatch_into(0, p_ref, x_ref, outs)

    def serve(r, previous):
        if r == 0:
            outs = call(
                first_kernel,
                "first_slot",
                [((STATE_ROWS + cap, 2 * width), BF16)] * INNER + [table] * 2,
                [IN_SMEM] + [IN_VMEM] * 6,
                spots,
                block,
                q,
                k,
                v,
                cot,
                cumul,
            )
        else:
            outs = call(
                next_kernel,
                "next_slot",
                [((cap, 2 * width), BF16)] * INNER + [table] * 2,
                [IN_SMEM, IN_VMEM],
                spots,
                blocks[r],
                needs=[previous],
            )
        sent[r] = exchange(outs[:INNER])
        tables[r] = outs[INNER:]
        return tables[r][0]

    def front(group, *needs):
        parts = [x for r in group for x in sent[r]]

        def kernel(*refs):
            front_kernel(cap, *refs)

        own = call(
            kernel,
            "expert_front",
            [((len(parts) * cap, hidden), BF16)] * 2,
            [IN_VMEM] * (len(parts) + 2),
            *parts,
            up_weights,
            down_weights,
            needs=needs,
        )
        if lax.axis_size("exp") == 2:
            other = [lax.ppermute(x, "exp", [(0, 1), (1, 0)]) for x in own]
            return own[0], [own[0], other[0], own[1], other[1]]
        return own[0], [lax.psum(x, "exp") for x in own]

    def finish(group, sums, previous):
        def kernel(*refs):
            back_kernel(len(group), cap, *refs)

        outs = call(
            kernel,
            "expert_back",
            [((len(group) * cap, width + META), BF16)] * INNER,
            [IN_SMEM] + [IN_VMEM] * (len(sums) + 1),
            where,
            *sums,
            up_weights,
            needs=[previous],
        )
        got = exchange(outs)
        for s, r in enumerate(group):
            answers[r] = (s * cap, got)
        return outs[0]

    def combine(r, previous):
        base, got = answers[r]
        last = r == 0

        def kernel(*refs, carried=bool(carry)):
            combine_kernel(base, carried, last, *refs)

        extra = carry + ([ids] if last else [])
        whole = ((tokens, width), BF16), ((top, tokens), BF16)
        outs = call(
            kernel,
            "combine",
            whole if last else [((tokens, width + META), BF16)],
            [IN_VMEM] * (2 + INNER + len(extra)),
            *tables[r],
            *got,
            *extra,
            needs=[previous],
        )
        if not last:
            carry[:] = [ring(outs[0])]
        return outs

    def plane_sums(previous):
        (total,) = call(
            plane_kernel,
            "plane_sums",
            [((STATE_ROWS, 2 * width), BF16)],
            [IN_SMEM] + [IN_VMEM] * INNER,
            spots,
            *sent[0],
            needs=[previous],
        )
        others.append(plane_flip(total, 1))
        return total

    def join(step, previous):
        last = 2 * step >= planes

        def kernel(*refs):
            join_kernel(last, *refs)

        (joined,) = call(
            kernel,
            "join_planes",
            [((STATE_ROWS, width if last else 2 * width), BF16)],
            [IN_SMEM] + [IN_VMEM] * (1 + len(others)),
            spots,
            plane_sum,
            *others,
            needs=[previous],
        )
        others.append(plane_flip(joined, step))
        return joined

    others = []
    previous = serve(0, None)
    previous = serve(1, previous)
    previous = plane_sum = plane_sums(previous)
    previous, sums = front([0, 1], previous)
    previous = serve(2, previous)
    previous = finish([0, 1], sums, previous)
    step = 2
    while step < planes:
        previous = join(step, previous)
        step *= 2
    previous, sums = front([2], previous)
    for r in range(3, planes):
        previous = finish([r - 1], sums, previous)
        previous = serve(r, previous)
        previous = combine(r - 2, previous)[0]
        previous, sums = front([r], previous, others[-1])
    previous = combine(planes - 2, previous)[0]
    previous = finish([planes - 1], sums, previous)
    previous = combine(planes - 1, previous)[0]
    states = call(
        spread_kernel,
        "spread_states",
        [((size // 2, width), BF16)] * INNER,
        [IN_SMEM] + [IN_VMEM] * (INNER + 1 + len(others)),
        spots,
        *sent[0],
        plane_sum,
        *others,
        needs=[previous],
    )
    states = exchange(states)
    grads = call(
        grads_kernel,
        "attention_grads",
        [(q.shape, BF16)] * 3,
        [IN_SMEM] + [IN_VMEM] * (5 + INNER),
        spots,
        q,
        k,
        v,
        cot,
        cumul,
        *states,
    )
    input_grad, gate_grad = combine(0, previous)
    return (*grads, input_grad, gate_grad.T)


def solution(mesh):
    rows = P("ctx", "exp")
    return jax.shard_map(
        body,
        mesh=mesh,
        in_specs=(
            rows,
            rows,
            rows,
            P("exp", "ctx"),
            rows,
            rows,
            P("ctx", None),
            P("ctx", None),
            P("ctx", "exp", None),
            P("ctx", None, "exp"),
        ),
        out_specs=(rows, rows, rows, rows, P("ctx", None)),
        check_vma=False,
    )
```

```python
import jax
import jax.numpy as jnp
from jax import lax
from jax.experimental import pallas as pl
from jax.experimental.pallas import tpu as pltpu
from jax.sharding import PartitionSpec as P

INNER = 4
META = 128
PAD = 8
STATE_ROWS = 40
F32 = jnp.float32
BF16 = jnp.bfloat16


def flip(x, m):
    n = lax.axis_size("ctx")
    return lax.ppermute(x, "ctx", [(i, i ^ m) for i in range(n)])


def exchange(parts):
    return [parts[0]] + [flip(parts[m], m) for m in range(1, INNER)]


def ring(x):
    n = lax.axis_size("ctx")
    return lax.ppermute(x, "ctx", [(i, (i + INNER) % n) for i in range(n)])


def unring(x):
    n = lax.axis_size("ctx")
    return lax.ppermute(x, "ctx", [(i, (i - INNER) % n) for i in range(n)])


def plane_flip(x, d):
    n = lax.axis_size("ctx")
    return lax.ppermute(x, "ctx", [(i, i ^ (INNER * d)) for i in range(n)])


def dot(a, b, ca, cb):
    return lax.dot_general(a, b, (((ca,), (cb,)), ((), ())), preferred_element_type=F32)


PARAMS = pltpu.CompilerParams(vmem_limit_bytes=28 * 1024 * 1024)
IN_SMEM = pl.BlockSpec(memory_space=pltpu.SMEM)
IN_VMEM = pl.BlockSpec(memory_space=pltpu.VMEM)
ANYWHERE = pl.BlockSpec(memory_space=pl.ANY)
IN_HBM = pl.BlockSpec(memory_space=pltpu.HBM)


def call(kernel, name, outs, specs, *args, scratch=(), needs=(), where=IN_VMEM):
    shapes = [jax.ShapeDtypeStruct(shape, dtype) for shape, dtype in outs]
    count, skip = len(args), len(needs)

    def run(*refs):
        kernel(*refs[:count], *refs[count + skip :])

    return pl.pallas_call(
        run,
        out_shape=shapes,
        in_specs=list(specs) + [ANYWHERE] * skip,
        out_specs=[where] * len(shapes),
        scratch_shapes=list(scratch),
        compiler_params=PARAMS,
        name=name,
    )(*args, *needs)


def split_rows(gain):
    high = gain.astype(BF16).astype(F32)
    mid = (gain - high).astype(BF16).astype(F32)
    low = gain - high - mid
    row = lax.broadcasted_iota(jnp.int32, (PAD, gain.shape[1]), 0)
    out = jnp.where(row == 0, high, jnp.where(row == 1, mid, jnp.where(row == 2, low, 0.0)))
    return out.astype(BF16)


def join_rows(rows):
    rows = rows.astype(F32)
    return rows[0:1] + rows[1:2] + rows[2:3]


def states_into(place, q_ref, k_ref, v_ref, c_ref, b_ref, outs):
    heads, length = b_ref.shape
    width = q_ref.shape[1]
    size = width // heads
    share = heads // INNER
    chunk = size // 4
    for m in range(INNER):
        for i in range(share):
            head = (place ^ m) * share + i
            cols = pl.ds(pl.multiple_of(head * size, size), size)
            decay = jnp.broadcast_to(b_ref[pl.ds(head, 1), :], (length, length)).T
            total = decay[length - 1 : length, :]
            scaled_k = (jnp.exp(total - decay) * k_ref[:, cols].astype(F32)).astype(BF16)
            scaled_q = (jnp.exp(decay) * q_ref[:, cols].astype(F32)).astype(BF16)
            state = dot(scaled_k, v_ref[:, cols], 0, 0).astype(BF16)
            adjoint = dot(scaled_q, c_ref[:, cols], 0, 0).astype(BF16)
            gains = split_rows(jnp.exp(total))
            for part in range(4):
                rows = slice(part * chunk, (part + 1) * chunk)
                left = slice((4 * i + part) * size, (4 * i + part + 1) * size)
                right = slice(width + (4 * i + part) * size, width + (4 * i + part + 1) * size)
                outs[m][0:chunk, left] = state[rows]
                outs[m][0:chunk, right] = adjoint[rows]
                outs[m][chunk:STATE_ROWS, left] = gains
                outs[m][chunk:STATE_ROWS, right] = gains


def plane_kernel(p_ref, x0, x1, x2, x3, out_ref):
    spots = [p_ref[0] ^ m for m in range(INNER)]
    xs = (x0, x1, x2, x3)
    width = out_ref.shape[1] // 2
    rows = STATE_ROWS - PAD
    gains = [join_rows(x[rows:STATE_ROWS, 0:width]) for x in xs]
    ones = jnp.ones_like(gains[0])
    up = jnp.zeros((rows, width), F32)
    down = jnp.zeros((rows, width), F32)
    for m in range(INNER):
        behind, before = ones, ones
        for j in range(INNER):
            behind = behind * jnp.where(spots[j] > spots[m], gains[j], ones)
            before = before * jnp.where(spots[j] < spots[m], gains[j], ones)
        up = up + behind * xs[m][0:rows, 0:width].astype(F32)
        down = down + before * xs[m][0:rows, width:].astype(F32)
    total = split_rows(gains[0] * gains[1] * gains[2] * gains[3])
    out_ref[0:rows, 0:width] = up.astype(BF16)
    out_ref[0:rows, width:] = down.astype(BF16)
    out_ref[rows:, 0:width] = total
    out_ref[rows:, width:] = total


def scan_planes(plane, own, others):
    width = own.shape[1] // 2
    rows = STATE_ROWS - PAD
    gain = join_rows(own[rows:, 0:width])
    ones = jnp.ones_like(gain)
    up = own[0:rows, 0:width].astype(F32)
    down = own[0:rows, width:].astype(F32)
    below = jnp.zeros_like(up)
    above = jnp.zeros_like(down)
    gain_below, gain_above = ones, ones
    for number, ref in enumerate(others):
        high = (plane & (1 << number)) != 0
        their_up = ref[0:rows, 0:width].astype(F32)
        their_down = ref[0:rows, width:].astype(F32)
        their_gain = join_rows(ref[rows:, 0:width])
        below = jnp.where(high, below + gain_below * their_up, below)
        gain_below = jnp.where(high, gain_below * their_gain, gain_below)
        above = jnp.where(high, above, above + gain_above * their_down)
        gain_above = jnp.where(high, gain_above, gain_above * their_gain)
        up = jnp.where(high, up + gain * their_up, their_up + their_gain * up)
        down = jnp.where(high, their_down + their_gain * down, down + gain * their_down)
        gain = gain * their_gain
    return up, down, gain, below, gain_below, above, gain_above


def join_kernel(last, p_ref, own, *refs):
    out_ref = refs[-1]
    plane = p_ref[1]
    rows = STATE_ROWS - PAD
    up, down, gain, *_ = scan_planes(plane, own, refs[:-1])
    if last:
        high = (plane & (1 << (len(refs) - 1))) != 0
        out_ref[0:rows, :] = jnp.where(high, down, up).astype(BF16)
        out_ref[rows:, :] = split_rows(gain)
        return
    width = up.shape[1]
    out_ref[0:rows, 0:width] = up.astype(BF16)
    out_ref[0:rows, width:] = down.astype(BF16)
    out_ref[rows:, 0:width] = split_rows(gain)
    out_ref[rows:, width:] = split_rows(gain)


def spread_kernel(p_ref, x0, x1, x2, x3, own, *refs):
    spots = [p_ref[0] ^ m for m in range(INNER)]
    plane = p_ref[1]
    xs, outs = (x0, x1, x2, x3), refs[-INNER:]
    others, final = refs[: -INNER - 1], refs[-INNER - 1]
    width = own.shape[1] // 2
    rows = STATE_ROWS - PAD
    gains = [join_rows(x[rows:STATE_ROWS, 0:width]) for x in xs]
    ones = jnp.ones_like(gains[0])
    zeros = jnp.zeros_like(gains[0])
    _, _, _, below, gain_below, above, gain_above = scan_planes(plane, own, others)
    high = (plane & (1 << len(others))) != 0
    far = final[0:rows, :].astype(F32)
    below = jnp.where(high, below + gain_below * far, below)
    above = jnp.where(high, above, above + gain_above * far)
    keys = [x[0:rows, 0:width].astype(F32) for x in xs]
    queries = [x[0:rows, width:].astype(F32) for x in xs]
    for m in range(INNER):
        first, last = ones, ones
        for j in range(INNER):
            first = first * jnp.where(spots[j] < spots[m], gains[j], ones)
            last = last * jnp.where(spots[j] > spots[m], gains[j], ones)
        state = first * below
        adjoint = last * above
        for i in range(INNER):
            if i == m:
                continue
            between = ones
            for j in range(INNER):
                if j == m or j == i:
                    continue
                inside = ((spots[j] > spots[i]) & (spots[j] < spots[m])) | (
                    (spots[j] < spots[i]) & (spots[j] > spots[m])
                )
                between = between * jnp.where(inside, gains[j], ones)
            state = state + jnp.where(spots[i] < spots[m], between, zeros) * keys[i]
            adjoint = adjoint + jnp.where(spots[i] > spots[m], between, zeros) * queries[i]
        outs[m][0:rows, :] = state.astype(BF16)
        outs[m][rows:, :] = adjoint.astype(BF16)


def decays(b_ref, head, length):
    across_rows = jnp.broadcast_to(b_ref[pl.ds(head, 1), :], (length, length))
    decay = across_rows.T
    return across_rows, decay, decay[length - 1 : length, :]


def inner_kernel(q_ref, k_ref, v_ref, c_ref, b_ref, dq_ref, dk_ref, dv_ref):
    heads, length = b_ref.shape
    size = q_ref.shape[1] // heads
    row = lax.broadcasted_iota(jnp.int32, (length, length), 0)
    col = lax.broadcasted_iota(jnp.int32, (length, length), 1)
    causal = row >= col
    for head in range(heads):
        cols = slice(head * size, (head + 1) * size)
        across_rows, decay, _ = decays(b_ref, head, length)
        mask = jnp.where(causal, jnp.exp(jnp.where(causal, decay - across_rows, 0.0)), 0.0)
        q, k, v, c = q_ref[:, cols], k_ref[:, cols], v_ref[:, cols], c_ref[:, cols]
        w = (dot(c, v, 1, 1) * mask).astype(BF16)
        z = (dot(q, k, 1, 1) * mask).astype(BF16)
        dq_ref[:, cols] = dot(w, k, 1, 0)
        dk_ref[:, cols] = dot(w, q, 0, 0)
        dv_ref[:, cols] = dot(z, c, 0, 0)


def outer_kernel(p_ref, k_ref, v_ref, c_ref, b_ref, eq_ref, ek_ref, ev_ref, s0, s1, s2, s3, *outs):
    place = p_ref[0]
    states = (s0, s1, s2, s3)
    dq_ref, dk_ref, dv_ref = outs
    heads, length = b_ref.shape
    size = k_ref.shape[1] // heads
    share = heads // INNER
    chunk = size // 4
    scale = 1.0 / size
    for m in range(INNER):
        quarter = place ^ m
        for i in range(share):
            head = quarter * share + i
            cols = pl.ds(pl.multiple_of(head * size, size), size)
            _, decay, total = decays(b_ref, head, length)
            lead = jnp.exp(decay)
            tail = jnp.exp(total - decay)
            k, v, c = k_ref[:, cols], v_ref[:, cols], c_ref[:, cols]
            tiles = [slice((4 * i + part) * size, (4 * i + part + 1) * size) for part in range(4)]
            state = jnp.concatenate([states[m][0:chunk, t] for t in tiles], axis=0)
            adjoint = jnp.concatenate([states[m][chunk : 2 * chunk, t] for t in tiles], axis=0)
            dq = eq_ref[:, cols] + lead * dot(c, state, 1, 1)
            dk = ek_ref[:, cols] + tail * dot(v, adjoint, 1, 1)
            dv = ev_ref[:, cols] + tail * dot(k, adjoint, 1, 0)
            dq_ref[:, cols] = (dq * scale).astype(BF16)
            dk_ref[:, cols] = (dk * scale).astype(BF16)
            dv_ref[:, cols] = (dv * scale).astype(BF16)


def pack_kernel(x_hbm, c_hbm, ids_hbm, gates_hbm, out_hbm, ids_ref, gates_ref, meta_ref, sems):
    tokens, width = x_hbm.shape
    top = ids_hbm.shape[0]
    pairs = [
        (ids_hbm, ids_ref),
        (gates_hbm, gates_ref),
        (x_hbm, out_hbm.at[:, 0:width]),
        (c_hbm, out_hbm.at[:, width : 2 * width]),
    ]
    copies = [pltpu.make_async_copy(a, b, sems.at[i]) for i, (a, b) in enumerate(pairs)]
    for copy in copies:
        copy.start()
    copies[0].wait()
    copies[1].wait()
    lists = [ids_ref[...].astype(F32), gates_ref[...].astype(F32)]
    lists.append(jnp.zeros((META - 2 * top, tokens), F32))
    meta_ref[...] = jnp.concatenate(lists, axis=0).T.astype(BF16)
    rest = pltpu.make_async_copy(meta_ref, out_hbm.at[:, 2 * width :], sems.at[4])
    rest.start()
    copies[2].wait()
    copies[3].wait()
    rest.wait()


def dispatch(block_ref, place, plane, cap, top):
    tokens, columns = block_ref.shape
    width = columns - META
    meta = block_ref[:, width:].astype(F32)
    j = lax.broadcasted_iota(jnp.int32, (tokens, INNER * cap), 1)
    part = jnp.zeros_like(j)
    for m in range(1, INNER):
        part = part + (j >= m * cap).astype(jnp.int32)
    expert = plane * INNER + (place ^ part)
    slots = (j - part * cap).astype(F32)
    expert = expert.astype(F32)
    named = jnp.zeros((tokens, INNER * cap), F32)
    weight = named
    for t in range(top):
        same = meta[:, t : t + 1] == expert
        named = jnp.where(same, 1.0, named)
        weight = jnp.where(same, meta[:, top + t : top + t + 1], weight)
    row = lax.broadcasted_iota(jnp.int32, (tokens, tokens), 0)
    col = lax.broadcasted_iota(jnp.int32, (tokens, tokens), 1)
    earlier = jnp.where(row > col, 1.0, 0.0).astype(BF16)
    rank = dot(earlier, named.astype(BF16), 1, 0)
    here = jnp.where(rank == slots, named, 0.0)
    weight = here * weight
    here = here.astype(BF16)
    rows = dot(here, block_ref[:, 0:width], 0, 0).astype(BF16)
    return rows, here, weight.astype(BF16)


def combine_kernel(base, carries, last, *refs):
    here_ref, weight_ref = refs[0:2]
    parts = refs[2 : 2 + INNER]
    cap = here_ref.shape[1] // INNER
    width = parts[0].shape[1] - META
    rows = jnp.concatenate([x[base : base + cap, :] for x in parts], axis=0)
    grads = dot(weight_ref[...], rows[:, 0:width], 1, 0)
    gates = dot(here_ref[...], rows[:, width:], 1, 0)
    for carry in refs[2 + INNER : 2 + INNER + carries]:
        grads = grads + carry[:, 0:width].astype(F32)
        gates = gates + carry[:, width:].astype(F32)
    if not last:
        refs[-1][:, 0:width] = grads.astype(BF16)
        refs[-1][:, width:] = gates.astype(BF16)
        return
    ids_ref, grad_ref, gate_ref = refs[-3:]
    grad_ref[...] = grads.astype(BF16)
    top, tokens = ids_ref.shape
    gates = gates.T
    row = lax.broadcasted_iota(jnp.int32, (META, tokens), 0)
    for t in range(top):
        mine = ids_ref[t : t + 1, :] == row
        picked = jnp.sum(jnp.where(mine, gates, 0.0), axis=0, keepdims=True)
        gate_ref[t : t + 1, :] = picked.astype(BF16)


def front_kernel(count, cap, *refs):
    parts, (up_ref, down_ref, pre_ref, back_ref) = refs[:-4], refs[-4:]
    width = up_ref.shape[1]
    rows = jnp.concatenate([x[x.shape[0] - cap :, :] for x in parts], axis=0)
    pre_ref[...] = dot(rows[:, 0:width], up_ref[0], 1, 0).astype(BF16)
    back_ref[...] = dot(rows[:, width:], down_ref[0], 1, 1).astype(BF16)


def back_kernel(slots, cap, i_ref, *refs):
    sums, up_ref, outs = refs[: -INNER - 1], refs[-INNER - 1], refs[-INNER:]
    width = up_ref.shape[1]
    half = len(sums) // 2
    totals = []
    for refs in (sums[:half], sums[half:]):
        terms = [ref[i].astype(F32) for ref in refs for i in range(ref.shape[0])]
        total = terms[0]
        for term in terms[1:]:
            total = total + term
        totals.append(total)
    pre, back = totals
    sig = 1.0 / (1.0 + jnp.exp(-pre))
    gate_back = jnp.sum(back * pre * sig, axis=1, keepdims=True)
    slope = (back * (sig * (1.0 + pre * (1.0 - sig)))).astype(BF16)
    lane = lax.broadcasted_iota(jnp.int32, (slope.shape[0], META), 1)
    gates = jnp.where(lane == i_ref[0], gate_back, 0.0).astype(BF16)
    grads = dot(slope, up_ref[0], 1, 1).astype(BF16)
    for s in range(slots):
        for m in range(INNER):
            source = slice((s * INNER + m) * cap, (s * INNER + m + 1) * cap)
            target = slice(s * cap, (s + 1) * cap)
            outs[m][target, 0:width] = grads[source]
            outs[m][target, width:] = gates[source]


def body(q, k, v, log_decay, cot, expert_input, router_gates, expert_ids, up_weights, down_weights):
    n = lax.axis_size("ctx")
    planes = n // INNER
    index = lax.axis_index("ctx").astype(jnp.int32)
    spots = jnp.stack([index % INNER, index // INNER])
    where = index.reshape(1)
    tokens, width = expert_input.shape
    top = expert_ids.shape[1]
    cap = 5 * tokens * top // (4 * n)
    heads = log_decay.shape[0]
    size = width // heads
    hidden = up_weights.shape[2]
    ids, gates = expert_ids.T, router_gates.T

    (block,) = call(
        pack_kernel,
        "pack",
        [((tokens, 2 * width + META), BF16)],
        [IN_HBM] * 4,
        *[pltpu.with_memory_space_constraint(x, pltpu.HBM) for x in (expert_input, cot, ids, gates)],
        scratch=[
            pltpu.VMEM((top, tokens), expert_ids.dtype),
            pltpu.VMEM((top, tokens), BF16),
            pltpu.VMEM((tokens, META), BF16),
            pltpu.SemaphoreType.DMA((5,)),
        ],
        where=IN_HBM,
    )
    blocks = [block]
    for _ in range(planes - 1):
        blocks.append(ring(blocks[-1]))

    row = lax.broadcasted_iota(jnp.int32, (tokens, tokens), 0)
    col = lax.broadcasted_iota(jnp.int32, (tokens, tokens), 1)
    cumul = jnp.dot(log_decay, (row <= col).astype(F32), precision=lax.Precision.HIGHEST)
    table = ((tokens, INNER * cap), BF16)
    sent, tables, answers, carry, direct = {}, {}, {}, [], []

    def dispatch_into(start, p_ref, x_ref, outs):
        rows, here, weight = dispatch(x_ref, p_ref[0], p_ref[1], cap, top)
        for m in range(INNER):
            outs[m][start:, :] = rows[m * cap : (m + 1) * cap]
        outs[INNER][...] = here
        outs[INNER + 1][...] = weight

    def first_kernel(p_ref, x_ref, q_ref, k_ref, v_ref, c_ref, b_ref, *outs):
        states_into(p_ref[0], q_ref, k_ref, v_ref, c_ref, b_ref, outs)
        dispatch_into(STATE_ROWS, p_ref, x_ref, outs)

    def next_kernel(p_ref, x_ref, *outs):
        dispatch_into(0, p_ref, x_ref, outs)

    def serve(r, previous):
        if r == 0:
            outs = call(
                first_kernel,
                "first_slot",
                [((STATE_ROWS + cap, 2 * width), BF16)] * INNER + [table] * 2,
                [IN_SMEM] + [IN_VMEM] * 6,
                spots,
                block,
                q,
                k,
                v,
                cot,
                cumul,
            )
        else:
            outs = call(
                next_kernel,
                "next_slot",
                [((cap, 2 * width), BF16)] * INNER + [table] * 2,
                [IN_SMEM, IN_VMEM],
                spots,
                blocks[r],
                needs=[previous],
            )
        sent[r] = exchange(outs[:INNER])
        tables[r] = outs[INNER:]
        return tables[r][0]

    def front(group, *needs):
        parts = [x for r in group for x in sent[r]]

        def kernel(*refs):
            front_kernel(len(group), cap, *refs)

        own = call(
            kernel,
            "expert_front",
            [((len(parts) * cap, hidden), BF16)] * 2,
            [IN_VMEM] * (len(parts) + 2),
            *parts,
            up_weights,
            down_weights,
            needs=needs,
        )
        if lax.axis_size("exp") == 2 and len(group) > 1:
            other = [lax.ppermute(x, "exp", [(0, 1), (1, 0)]) for x in own]
            return own[0], [own[0][None], other[0][None], own[1][None], other[1][None]]
        return own[0], [lax.all_gather(x, "exp") for x in own]

    def finish(group, sums, *needs):
        def kernel(*refs):
            back_kernel(len(group), cap, *refs)

        outs = call(
            kernel,
            "expert_back",
            [((len(group) * cap, width + META), BF16)] * INNER,
            [IN_SMEM] + [IN_VMEM] * (len(sums) + 1),
            where,
            *sums,
            up_weights,
            needs=needs,
        )
        got = exchange(outs)
        for s, r in enumerate(group):
            answers[r] = (s * cap, got)
        return outs[0]

    def combine(r, *needs):
        base, got = answers[r]
        last = r == 0

        if last:
            carry.extend(direct)

        def kernel(*refs, carried=len(carry)):
            combine_kernel(base, carried, last, *refs)

        extra = carry + ([ids] if last else [])
        whole = ((tokens, width), BF16), ((top, tokens), BF16)
        outs = call(
            kernel,
            "combine",
            whole if last else [((tokens, width + META), BF16)],
            [IN_VMEM] * (2 + INNER + len(extra)),
            *tables[r],
            *got,
            *extra,
            needs=needs,
        )
        if r == 1:
            direct.append(unring(outs[0]))
        elif not last:
            carry[:] = [ring(outs[0])]
        return outs

    def plane_sums(previous):
        (total,) = call(
            plane_kernel,
            "plane_sums",
            [((STATE_ROWS, 2 * width), BF16)],
            [IN_SMEM] + [IN_VMEM] * INNER,
            spots,
            *sent[0],
            needs=[previous],
        )
        others.append(plane_flip(total, 1))
        return total

    def join(step, previous):
        last = 2 * step >= planes

        def kernel(*refs):
            join_kernel(last, *refs)

        (joined,) = call(
            kernel,
            "join_planes",
            [((STATE_ROWS, width if last else 2 * width), BF16)],
            [IN_SMEM] + [IN_VMEM] * (1 + len(others)),
            spots,
            plane_sum,
            *others,
            needs=[previous],
        )
        others.append(plane_flip(joined, step))
        return joined

    others = []
    previous = serve(0, None)
    early = call(
        inner_kernel,
        "inner_grads",
        [(q.shape, F32)] * 3,
        [IN_VMEM] * 5,
        q,
        k,
        v,
        cot,
        cumul,
        needs=[previous],
    )
    previous = serve(1, early[0])
    previous, sums = front([0, 1], previous)
    previous = serve(2, previous)
    previous = finish([0, 1], sums, previous)
    previous = plane_sum = plane_sums(previous)
    previous, sums = front([2], previous)
    for r in range(3, planes):
        previous = finish([r - 1], sums, previous)
        previous = combine(r - 2, previous, others[0])[0]
        previous = serve(r, previous)
        if r == 3:
            step = 2
            while step < planes:
                previous = join(step, previous)
                step *= 2
        previous, sums = front([r], previous, *direct)
    previous = finish([planes - 1], sums, previous, others[-1])
    previous = combine(planes - 2, previous)[0]
    states = call(
        spread_kernel,
        "spread_states",
        [((size // 2, width), BF16)] * INNER,
        [IN_SMEM] + [IN_VMEM] * (INNER + 1 + len(others)),
        spots,
        *sent[0],
        plane_sum,
        *others,
        needs=[previous],
    )
    previous = combine(planes - 1, states[0])[0]
    states = exchange(states)
    grads = call(
        outer_kernel,
        "outer_grads",
        [(q.shape, BF16)] * 3,
        [IN_SMEM] + [IN_VMEM] * (7 + INNER),
        spots,
        k,
        v,
        cot,
        cumul,
        *early,
        *states,
        needs=[previous],
    )
    input_grad, gate_grad = combine(0, grads[0])
    return (*grads, input_grad, gate_grad.T)


def solution(mesh):
    rows = P("ctx", "exp")
    return jax.shard_map(
        body,
        mesh=mesh,
        in_specs=(
            rows,
            rows,
            rows,
            P("exp", "ctx"),
            rows,
            rows,
            P("ctx", None),
            P("ctx", None),
            P("ctx", "exp", None),
            P("ctx", None, "exp"),
        ),
        out_specs=(rows, rows, rows, rows, P("ctx", None)),
        check_vma=False,
    )
```

```python
import jax
import jax.numpy as jnp
from jax import lax
from jax.experimental import pallas as pl
from jax.experimental.pallas import tpu as pltpu
from jax.sharding import PartitionSpec as P

INNER = 4
META = 128
PAD = 8
STATE_ROWS = 40
F32 = jnp.float32
BF16 = jnp.bfloat16


def flip(x, m):
    n = lax.axis_size("ctx")
    return lax.ppermute(x, "ctx", [(i, i ^ m) for i in range(n)])


def exchange(parts):
    return [parts[0]] + [flip(parts[m], m) for m in range(1, INNER)]


def ring(x):
    n = lax.axis_size("ctx")
    return lax.ppermute(x, "ctx", [(i, (i + INNER) % n) for i in range(n)])


def unring(x):
    n = lax.axis_size("ctx")
    return lax.ppermute(x, "ctx", [(i, (i - INNER) % n) for i in range(n)])


def plane_flip(x, d):
    n = lax.axis_size("ctx")
    return lax.ppermute(x, "ctx", [(i, i ^ (INNER * d)) for i in range(n)])


def dot(a, b, ca, cb):
    return lax.dot_general(a, b, (((ca,), (cb,)), ((), ())), preferred_element_type=F32)


PARAMS = pltpu.CompilerParams(vmem_limit_bytes=28 * 1024 * 1024)
IN_SMEM = pl.BlockSpec(memory_space=pltpu.SMEM)
IN_VMEM = pl.BlockSpec(memory_space=pltpu.VMEM)
ANYWHERE = pl.BlockSpec(memory_space=pl.ANY)
IN_HBM = pl.BlockSpec(memory_space=pltpu.HBM)


def call(kernel, name, outs, specs, *args, scratch=(), needs=(), where=IN_VMEM):
    shapes = [jax.ShapeDtypeStruct(shape, dtype) for shape, dtype in outs]
    count, skip = len(args), len(needs)

    def run(*refs):
        kernel(*refs[:count], *refs[count + skip :])

    return pl.pallas_call(
        run,
        out_shape=shapes,
        in_specs=list(specs) + [ANYWHERE] * skip,
        out_specs=[where] * len(shapes),
        scratch_shapes=list(scratch),
        compiler_params=PARAMS,
        name=name,
    )(*args, *needs)


def split_rows(gain):
    high = gain.astype(BF16).astype(F32)
    mid = (gain - high).astype(BF16).astype(F32)
    low = gain - high - mid
    row = lax.broadcasted_iota(jnp.int32, (PAD, gain.shape[1]), 0)
    out = jnp.where(row == 0, high, jnp.where(row == 1, mid, jnp.where(row == 2, low, 0.0)))
    return out.astype(BF16)


def join_rows(rows):
    rows = rows.astype(F32)
    return rows[0:1] + rows[1:2] + rows[2:3]


def states_into(place, q_ref, k_ref, v_ref, c_ref, b_ref, outs):
    heads, length = b_ref.shape
    width = q_ref.shape[1]
    size = width // heads
    share = heads // INNER
    chunk = size // 4
    for m in range(INNER):
        for i in range(share):
            head = (place ^ m) * share + i
            cols = pl.ds(pl.multiple_of(head * size, size), size)
            decay = jnp.broadcast_to(b_ref[pl.ds(head, 1), :], (length, length)).T
            total = decay[length - 1 : length, :]
            scaled_k = (jnp.exp(total - decay) * k_ref[:, cols].astype(F32)).astype(BF16)
            scaled_q = (jnp.exp(decay) * q_ref[:, cols].astype(F32)).astype(BF16)
            state = dot(scaled_k, v_ref[:, cols], 0, 0).astype(BF16)
            adjoint = dot(scaled_q, c_ref[:, cols], 0, 0).astype(BF16)
            gains = split_rows(jnp.exp(total))
            for part in range(4):
                rows = slice(part * chunk, (part + 1) * chunk)
                left = slice((4 * i + part) * size, (4 * i + part + 1) * size)
                right = slice(width + (4 * i + part) * size, width + (4 * i + part + 1) * size)
                outs[m][0:chunk, left] = state[rows]
                outs[m][0:chunk, right] = adjoint[rows]
                outs[m][chunk:STATE_ROWS, left] = gains
                outs[m][chunk:STATE_ROWS, right] = gains


def plane_kernel(p_ref, x0, x1, x2, x3, out_ref):
    spots = [p_ref[0] ^ m for m in range(INNER)]
    xs = (x0, x1, x2, x3)
    width = out_ref.shape[1] // 2
    rows = STATE_ROWS - PAD
    gains = [join_rows(x[rows:STATE_ROWS, 0:width]) for x in xs]
    ones = jnp.ones_like(gains[0])
    up = jnp.zeros((rows, width), F32)
    down = jnp.zeros((rows, width), F32)
    for m in range(INNER):
        behind, before = ones, ones
        for j in range(INNER):
            behind = behind * jnp.where(spots[j] > spots[m], gains[j], ones)
            before = before * jnp.where(spots[j] < spots[m], gains[j], ones)
        up = up + behind * xs[m][0:rows, 0:width].astype(F32)
        down = down + before * xs[m][0:rows, width:].astype(F32)
    total = split_rows(gains[0] * gains[1] * gains[2] * gains[3])
    out_ref[0:rows, 0:width] = up.astype(BF16)
    out_ref[0:rows, width:] = down.astype(BF16)
    out_ref[rows:, 0:width] = total
    out_ref[rows:, width:] = total


def scan_planes(plane, own, others):
    width = own.shape[1] // 2
    rows = STATE_ROWS - PAD
    gain = join_rows(own[rows:, 0:width])
    ones = jnp.ones_like(gain)
    up = own[0:rows, 0:width].astype(F32)
    down = own[0:rows, width:].astype(F32)
    below = jnp.zeros_like(up)
    above = jnp.zeros_like(down)
    gain_below, gain_above = ones, ones
    for number, ref in enumerate(others):
        high = (plane & (1 << number)) != 0
        their_up = ref[0:rows, 0:width].astype(F32)
        their_down = ref[0:rows, width:].astype(F32)
        their_gain = join_rows(ref[rows:, 0:width])
        below = jnp.where(high, below + gain_below * their_up, below)
        gain_below = jnp.where(high, gain_below * their_gain, gain_below)
        above = jnp.where(high, above, above + gain_above * their_down)
        gain_above = jnp.where(high, gain_above, gain_above * their_gain)
        up = jnp.where(high, up + gain * their_up, their_up + their_gain * up)
        down = jnp.where(high, their_down + their_gain * down, down + gain * their_down)
        gain = gain * their_gain
    return up, down, gain, below, gain_below, above, gain_above


def join_kernel(last, p_ref, own, *refs):
    out_ref = refs[-1]
    plane = p_ref[1]
    rows = STATE_ROWS - PAD
    up, down, gain, *_ = scan_planes(plane, own, refs[:-1])
    if last:
        high = (plane & (1 << (len(refs) - 1))) != 0
        out_ref[0:rows, :] = jnp.where(high, down, up).astype(BF16)
        out_ref[rows:, :] = split_rows(gain)
        return
    width = up.shape[1]
    out_ref[0:rows, 0:width] = up.astype(BF16)
    out_ref[0:rows, width:] = down.astype(BF16)
    out_ref[rows:, 0:width] = split_rows(gain)
    out_ref[rows:, width:] = split_rows(gain)


def spread_kernel(p_ref, x0, x1, x2, x3, own, *refs):
    spots = [p_ref[0] ^ m for m in range(INNER)]
    plane = p_ref[1]
    xs, outs = (x0, x1, x2, x3), refs[-INNER:]
    others, final = refs[: -INNER - 1], refs[-INNER - 1]
    width = own.shape[1] // 2
    rows = STATE_ROWS - PAD
    gains = [join_rows(x[rows:STATE_ROWS, 0:width]) for x in xs]
    ones = jnp.ones_like(gains[0])
    zeros = jnp.zeros_like(gains[0])
    _, _, _, below, gain_below, above, gain_above = scan_planes(plane, own, others)
    high = (plane & (1 << len(others))) != 0
    far = final[0:rows, :].astype(F32)
    below = jnp.where(high, below + gain_below * far, below)
    above = jnp.where(high, above, above + gain_above * far)
    keys = [x[0:rows, 0:width].astype(F32) for x in xs]
    queries = [x[0:rows, width:].astype(F32) for x in xs]
    for m in range(INNER):
        first, last = ones, ones
        for j in range(INNER):
            first = first * jnp.where(spots[j] < spots[m], gains[j], ones)
            last = last * jnp.where(spots[j] > spots[m], gains[j], ones)
        state = first * below
        adjoint = last * above
        for i in range(INNER):
            if i == m:
                continue
            between = ones
            for j in range(INNER):
                if j == m or j == i:
                    continue
                inside = ((spots[j] > spots[i]) & (spots[j] < spots[m])) | (
                    (spots[j] < spots[i]) & (spots[j] > spots[m])
                )
                between = between * jnp.where(inside, gains[j], ones)
            state = state + jnp.where(spots[i] < spots[m], between, zeros) * keys[i]
            adjoint = adjoint + jnp.where(spots[i] > spots[m], between, zeros) * queries[i]
        outs[m][0:rows, :] = state.astype(BF16)
        outs[m][rows:, :] = adjoint.astype(BF16)


def decays(b_ref, head, length):
    across_rows = jnp.broadcast_to(b_ref[pl.ds(head, 1), :], (length, length))
    decay = across_rows.T
    return across_rows, decay, decay[length - 1 : length, :]


def inner_kernel(q_ref, k_ref, v_ref, c_ref, b_ref, dq_ref, dk_ref, dv_ref, flag_ref):
    flag_ref[...] = jnp.zeros_like(flag_ref)
    heads, length = b_ref.shape
    size = q_ref.shape[1] // heads
    row = lax.broadcasted_iota(jnp.int32, (length, length), 0)
    col = lax.broadcasted_iota(jnp.int32, (length, length), 1)
    causal = row >= col
    for head in range(heads):
        cols = slice(head * size, (head + 1) * size)
        across_rows, decay, _ = decays(b_ref, head, length)
        mask = jnp.where(causal, jnp.exp(jnp.where(causal, decay - across_rows, 0.0)), 0.0)
        q, k, v, c = q_ref[:, cols], k_ref[:, cols], v_ref[:, cols], c_ref[:, cols]
        w = (dot(c, v, 1, 1) * mask).astype(BF16)
        z = (dot(q, k, 1, 1) * mask).astype(BF16)
        dq_ref[:, cols] = dot(w, k, 1, 0)
        dk_ref[:, cols] = dot(w, q, 0, 0)
        dv_ref[:, cols] = dot(z, c, 0, 0)


def outer_kernel(p_ref, k_ref, v_ref, c_ref, b_ref, eq_ref, ek_ref, ev_ref, s0, s1, s2, s3, *outs):
    place = p_ref[0]
    states = (s0, s1, s2, s3)
    dq_ref, dk_ref, dv_ref, flag_ref = outs
    flag_ref[...] = jnp.zeros_like(flag_ref)
    heads, length = b_ref.shape
    size = k_ref.shape[1] // heads
    share = heads // INNER
    chunk = size // 4
    scale = 1.0 / size
    for m in range(INNER):
        quarter = place ^ m
        for i in range(share):
            head = quarter * share + i
            cols = pl.ds(pl.multiple_of(head * size, size), size)
            _, decay, total = decays(b_ref, head, length)
            lead = jnp.exp(decay)
            tail = jnp.exp(total - decay)
            k, v, c = k_ref[:, cols], v_ref[:, cols], c_ref[:, cols]
            tiles = [slice((4 * i + part) * size, (4 * i + part + 1) * size) for part in range(4)]
            state = jnp.concatenate([states[m][0:chunk, t] for t in tiles], axis=0)
            adjoint = jnp.concatenate([states[m][chunk : 2 * chunk, t] for t in tiles], axis=0)
            dq = eq_ref[:, cols] + lead * dot(c, state, 1, 1)
            dk = ek_ref[:, cols] + tail * dot(v, adjoint, 1, 1)
            dv = ev_ref[:, cols] + tail * dot(k, adjoint, 1, 0)
            dq_ref[:, cols] = (dq * scale).astype(BF16)
            dk_ref[:, cols] = (dk * scale).astype(BF16)
            dv_ref[:, cols] = (dv * scale).astype(BF16)


def pack_kernel(x_hbm, c_hbm, ids_hbm, gates_hbm, out_hbm, ids_ref, gates_ref, meta_ref, sems):
    tokens, width = x_hbm.shape
    top = ids_hbm.shape[0]
    pairs = [
        (ids_hbm, ids_ref),
        (gates_hbm, gates_ref),
        (x_hbm, out_hbm.at[:, 0:width]),
        (c_hbm, out_hbm.at[:, width : 2 * width]),
    ]
    copies = [pltpu.make_async_copy(a, b, sems.at[i]) for i, (a, b) in enumerate(pairs)]
    for copy in copies:
        copy.start()
    copies[0].wait()
    copies[1].wait()
    lists = [ids_ref[...].astype(F32), gates_ref[...].astype(F32)]
    lists.append(jnp.zeros((META - 2 * top, tokens), F32))
    meta_ref[...] = jnp.concatenate(lists, axis=0).T.astype(BF16)
    rest = pltpu.make_async_copy(meta_ref, out_hbm.at[:, 2 * width :], sems.at[4])
    rest.start()
    copies[2].wait()
    copies[3].wait()
    rest.wait()


def dispatch(block_ref, place, plane, cap, top):
    tokens, columns = block_ref.shape
    width = columns - META
    meta = block_ref[:, width:].astype(F32)
    j = lax.broadcasted_iota(jnp.int32, (tokens, INNER * cap), 1)
    part = jnp.zeros_like(j)
    for m in range(1, INNER):
        part = part + (j >= m * cap).astype(jnp.int32)
    expert = plane * INNER + (place ^ part)
    slots = (j - part * cap).astype(F32)
    expert = expert.astype(F32)
    named = jnp.zeros((tokens, INNER * cap), F32)
    weight = named
    for t in range(top):
        same = meta[:, t : t + 1] == expert
        named = jnp.where(same, 1.0, named)
        weight = jnp.where(same, meta[:, top + t : top + t + 1], weight)
    row = lax.broadcasted_iota(jnp.int32, (tokens, tokens), 0)
    col = lax.broadcasted_iota(jnp.int32, (tokens, tokens), 1)
    earlier = jnp.where(row > col, 1.0, 0.0).astype(BF16)
    rank = dot(earlier, named.astype(BF16), 1, 0)
    here = jnp.where(rank == slots, named, 0.0)
    weight = here * weight
    here = here.astype(BF16)
    rows = dot(here, block_ref[:, 0:width], 0, 0).astype(BF16)
    return rows, here, weight.astype(BF16)


def combine_kernel(base, carries, last, *refs):
    here_ref, weight_ref = refs[0:2]
    parts = refs[2 : 2 + INNER]
    cap = here_ref.shape[1] // INNER
    width = parts[0].shape[1] - META
    rows = jnp.concatenate([x[base : base + cap, :] for x in parts], axis=0)
    grads = dot(weight_ref[...], rows[:, 0:width], 1, 0)
    gates = dot(here_ref[...], rows[:, width:], 1, 0)
    for carry in refs[2 + INNER : 2 + INNER + carries]:
        grads = grads + carry[:, 0:width].astype(F32)
        gates = gates + carry[:, width:].astype(F32)
    if not last:
        refs[-1][:, 0:width] = grads.astype(BF16)
        refs[-1][:, width:] = gates.astype(BF16)
        return
    ids_ref, grad_ref, gate_ref = refs[-3:]
    grad_ref[...] = grads.astype(BF16)
    top, tokens = ids_ref.shape
    gates = gates.T
    row = lax.broadcasted_iota(jnp.int32, (META, tokens), 0)
    for t in range(top):
        mine = ids_ref[t : t + 1, :] == row
        picked = jnp.sum(jnp.where(mine, gates, 0.0), axis=0, keepdims=True)
        gate_ref[t : t + 1, :] = picked.astype(BF16)


def front_kernel(count, cap, *refs):
    parts, (up_ref, down_ref, pre_ref, back_ref) = refs[:-4], refs[-4:]
    width = up_ref.shape[1]
    rows = jnp.concatenate([x[x.shape[0] - cap :, :] for x in parts], axis=0)
    pre_ref[...] = dot(rows[:, 0:width], up_ref[0], 1, 0).astype(BF16)
    back_ref[...] = dot(rows[:, width:], down_ref[0], 1, 1).astype(BF16)


def back_kernel(slots, cap, i_ref, *refs):
    sums, up_ref, outs = refs[: -INNER - 1], refs[-INNER - 1], refs[-INNER:]
    width = up_ref.shape[1]
    half = len(sums) // 2
    totals = []
    for refs in (sums[:half], sums[half:]):
        terms = [ref[i].astype(F32) for ref in refs for i in range(ref.shape[0])]
        total = terms[0]
        for term in terms[1:]:
            total = total + term
        totals.append(total)
    pre, back = totals
    sig = 1.0 / (1.0 + jnp.exp(-pre))
    gate_back = jnp.sum(back * pre * sig, axis=1, keepdims=True)
    slope = (back * (sig * (1.0 + pre * (1.0 - sig)))).astype(BF16)
    lane = lax.broadcasted_iota(jnp.int32, (slope.shape[0], META), 1)
    gates = jnp.where(lane == i_ref[0], gate_back, 0.0).astype(BF16)
    grads = dot(slope, up_ref[0], 1, 1).astype(BF16)
    for s in range(slots):
        for m in range(INNER):
            source = slice((s * INNER + m) * cap, (s * INNER + m + 1) * cap)
            target = slice(s * cap, (s + 1) * cap)
            outs[m][target, 0:width] = grads[source]
            outs[m][target, width:] = gates[source]


def body(q, k, v, log_decay, cot, expert_input, router_gates, expert_ids, up_weights, down_weights):
    n = lax.axis_size("ctx")
    planes = n // INNER
    index = lax.axis_index("ctx").astype(jnp.int32)
    spots = jnp.stack([index % INNER, index // INNER])
    where = index.reshape(1)
    tokens, width = expert_input.shape
    top = expert_ids.shape[1]
    cap = 5 * tokens * top // (4 * n)
    heads = log_decay.shape[0]
    size = width // heads
    hidden = up_weights.shape[2]
    ids, gates = expert_ids.T, router_gates.T

    (block,) = call(
        pack_kernel,
        "pack",
        [((tokens, 2 * width + META), BF16)],
        [IN_HBM] * 4,
        *[pltpu.with_memory_space_constraint(x, pltpu.HBM) for x in (expert_input, cot, ids, gates)],
        scratch=[
            pltpu.VMEM((top, tokens), expert_ids.dtype),
            pltpu.VMEM((top, tokens), BF16),
            pltpu.VMEM((tokens, META), BF16),
            pltpu.SemaphoreType.DMA((5,)),
        ],
        where=IN_HBM,
    )
    blocks = [block]
    for _ in range(planes - 1):
        blocks.append(ring(blocks[-1]))

    row = lax.broadcasted_iota(jnp.int32, (tokens, tokens), 0)
    col = lax.broadcasted_iota(jnp.int32, (tokens, tokens), 1)
    cumul = jnp.dot(log_decay, (row <= col).astype(F32), precision=lax.Precision.HIGHEST)
    table = ((tokens, INNER * cap), BF16)
    sent, tables, answers, carry, direct = {}, {}, {}, [], []

    def dispatch_into(start, p_ref, x_ref, outs):
        rows, here, weight = dispatch(x_ref, p_ref[0], p_ref[1], cap, top)
        for m in range(INNER):
            outs[m][start:, :] = rows[m * cap : (m + 1) * cap]
        outs[INNER][...] = here
        outs[INNER + 1][...] = weight

    def first_kernel(p_ref, x_ref, q_ref, k_ref, v_ref, c_ref, b_ref, *outs):
        states_into(p_ref[0], q_ref, k_ref, v_ref, c_ref, b_ref, outs)
        dispatch_into(STATE_ROWS, p_ref, x_ref, outs)

    def next_kernel(p_ref, x_ref, *outs):
        dispatch_into(0, p_ref, x_ref, outs)

    def serve(r, previous):
        if r == 0:
            outs = call(
                first_kernel,
                "first_slot",
                [((STATE_ROWS + cap, 2 * width), BF16)] * INNER + [table] * 2,
                [IN_SMEM] + [IN_VMEM] * 6,
                spots,
                block,
                q,
                k,
                v,
                cot,
                cumul,
            )
        else:
            outs = call(
                next_kernel,
                "next_slot",
                [((cap, 2 * width), BF16)] * INNER + [table] * 2,
                [IN_SMEM, IN_VMEM],
                spots,
                blocks[r],
                needs=[previous],
            )
        sent[r] = exchange(outs[:INNER])
        tables[r] = outs[INNER:]
        return tables[r][0]

    def front(group, *needs):
        parts = [x for r in group for x in sent[r]]

        def kernel(*refs):
            front_kernel(len(group), cap, *refs)

        own = call(
            kernel,
            "expert_front",
            [((len(parts) * cap, hidden), BF16)] * 2,
            [IN_VMEM] * (len(parts) + 2),
            *parts,
            up_weights,
            down_weights,
            needs=needs,
        )
        if lax.axis_size("exp") == 2 and len(group) > 1:
            other = [lax.ppermute(x, "exp", [(0, 1), (1, 0)]) for x in own]
            return own[0], [own[0][None], other[0][None], own[1][None], other[1][None]]
        return own[0], [lax.all_gather(x, "exp") for x in own]

    def finish(group, sums, *needs):
        def kernel(*refs):
            back_kernel(len(group), cap, *refs)

        outs = call(
            kernel,
            "expert_back",
            [((len(group) * cap, width + META), BF16)] * INNER,
            [IN_SMEM] + [IN_VMEM] * (len(sums) + 1),
            where,
            *sums,
            up_weights,
            needs=needs,
        )
        got = exchange(outs)
        for s, r in enumerate(group):
            answers[r] = (s * cap, got)
        return outs[0]

    def combine(r, *needs):
        base, got = answers[r]
        last = r == 0

        if last:
            carry.extend(direct)

        def kernel(*refs, carried=len(carry)):
            combine_kernel(base, carried, last, *refs)

        extra = carry + ([ids] if last else [])
        whole = ((tokens, width), BF16), ((top, tokens), BF16)
        outs = call(
            kernel,
            "combine",
            whole if last else [((tokens, width + META), BF16)],
            [IN_VMEM] * (2 + INNER + len(extra)),
            *tables[r],
            *got,
            *extra,
            needs=needs,
        )
        if r == 1:
            direct.append(unring(outs[0]))
        elif not last:
            carry[:] = [ring(outs[0])]
        return outs

    def plane_sums(previous):
        (total,) = call(
            plane_kernel,
            "plane_sums",
            [((STATE_ROWS, 2 * width), BF16)],
            [IN_SMEM] + [IN_VMEM] * INNER,
            spots,
            *sent[0],
            needs=[previous],
        )
        others.append(plane_flip(total, 1))
        return total

    def join(step, previous):
        last = 2 * step >= planes

        def kernel(*refs):
            join_kernel(last, *refs)

        (joined,) = call(
            kernel,
            "join_planes",
            [((STATE_ROWS, width if last else 2 * width), BF16)],
            [IN_SMEM] + [IN_VMEM] * (1 + len(others)),
            spots,
            plane_sum,
            *others,
            needs=[previous],
        )
        others.append(plane_flip(joined, step))
        return joined

    others = []
    previous = serve(0, None)
    early = call(
        inner_kernel,
        "inner_grads",
        [(q.shape, F32)] * 3 + [((8, 128), F32)],
        [IN_VMEM] * 5,
        q,
        k,
        v,
        cot,
        cumul,
        needs=[previous],
    )
    previous = serve(1, early[3])
    previous, sums = front([0, 1], previous)
    previous = serve(2, previous)
    previous = finish([0, 1], sums, previous)
    previous = plane_sum = plane_sums(previous)
    previous, sums = front([2], previous)
    for r in range(3, planes):
        previous = finish([r - 1], sums, previous)
        previous = combine(r - 2, previous, others[0])[0]
        previous = serve(r, previous)
        if r == 3:
            step = 2
            while step < planes:
                previous = join(step, previous)
                step *= 2
        previous, sums = front([r], previous, *direct)
        if r == planes - 1:
            previous = combine(planes - 2, previous)[0]
    previous = finish([planes - 1], sums, previous, others[-1])
    states = call(
        spread_kernel,
        "spread_states",
        [((size // 2, width), BF16)] * INNER,
        [IN_SMEM] + [IN_VMEM] * (INNER + 1 + len(others)),
        spots,
        *sent[0],
        plane_sum,
        *others,
        needs=[previous],
    )
    previous = combine(planes - 1, states[0])[0]
    states = exchange(states)
    grads = call(
        outer_kernel,
        "outer_grads",
        [(q.shape, BF16)] * 3 + [((8, 128), F32)],
        [IN_SMEM] + [IN_VMEM] * (7 + INNER),
        spots,
        k,
        v,
        cot,
        cumul,
        *early[:3],
        *states,
        needs=[previous],
    )
    input_grad, gate_grad = combine(0, grads[3])
    return (*grads[:3], input_grad, gate_grad.T)


def solution(mesh):
    rows = P("ctx", "exp")
    return jax.shard_map(
        body,
        mesh=mesh,
        in_specs=(
            rows,
            rows,
            rows,
            P("exp", "ctx"),
            rows,
            rows,
            P("ctx", None),
            P("ctx", None),
            P("ctx", "exp", None),
            P("ctx", None, "exp"),
        ),
        out_specs=(rows, rows, rows, rows, P("ctx", None)),
        check_vma=False,
    )
```

```python
import jax
import jax.numpy as jnp
from jax import lax
from jax.experimental import pallas as pl
from jax.experimental.pallas import tpu as pltpu
from jax.sharding import PartitionSpec as P

INNER = 4
META = 128
PAD = 8
STATE_ROWS = 40
F32 = jnp.float32
BF16 = jnp.bfloat16


def flip(x, m):
    n = lax.axis_size("ctx")
    return lax.ppermute(x, "ctx", [(i, i ^ m) for i in range(n)])


def exchange(parts):
    return [parts[0]] + [flip(parts[m], m) for m in range(1, INNER)]


def ring(x):
    n = lax.axis_size("ctx")
    return lax.ppermute(x, "ctx", [(i, (i + INNER) % n) for i in range(n)])


def unring(x):
    n = lax.axis_size("ctx")
    return lax.ppermute(x, "ctx", [(i, (i - INNER) % n) for i in range(n)])


def plane_flip(x, d):
    n = lax.axis_size("ctx")
    return lax.ppermute(x, "ctx", [(i, i ^ (INNER * d)) for i in range(n)])


def dot(a, b, ca, cb):
    return lax.dot_general(a, b, (((ca,), (cb,)), ((), ())), preferred_element_type=F32)


PARAMS = pltpu.CompilerParams(vmem_limit_bytes=20 * 1024 * 1024)
IN_SMEM = pl.BlockSpec(memory_space=pltpu.SMEM)
IN_VMEM = pl.BlockSpec(memory_space=pltpu.VMEM)
ANYWHERE = pl.BlockSpec(memory_space=pl.ANY)
IN_HBM = pl.BlockSpec(memory_space=pltpu.HBM)


def call(kernel, name, outs, specs, *args, scratch=(), needs=(), where=IN_VMEM):
    shapes = [jax.ShapeDtypeStruct(shape, dtype) for shape, dtype in outs]
    count, skip = len(args), len(needs)

    def run(*refs):
        kernel(*refs[:count], *refs[count + skip :])

    return pl.pallas_call(
        run,
        out_shape=shapes,
        in_specs=list(specs) + [ANYWHERE] * skip,
        out_specs=[where] * len(shapes),
        scratch_shapes=list(scratch),
        compiler_params=PARAMS,
        name=name,
    )(*args, *needs)


def split_rows(gain):
    high = gain.astype(BF16).astype(F32)
    mid = (gain - high).astype(BF16).astype(F32)
    low = gain - high - mid
    row = lax.broadcasted_iota(jnp.int32, (PAD, gain.shape[1]), 0)
    out = jnp.where(row == 0, high, jnp.where(row == 1, mid, jnp.where(row == 2, low, 0.0)))
    return out.astype(BF16)


def join_rows(rows):
    rows = rows.astype(F32)
    return rows[0:1] + rows[1:2] + rows[2:3]


def states_into(place, q_ref, k_ref, v_ref, c_ref, b_ref, outs):
    heads, length = b_ref.shape
    width = q_ref.shape[1]
    size = width // heads
    share = heads // INNER
    chunk = size // 4
    for m in range(INNER):
        for i in range(share):
            head = (place ^ m) * share + i
            cols = pl.ds(pl.multiple_of(head * size, size), size)
            decay = jnp.broadcast_to(b_ref[pl.ds(head, 1), :], (length, length)).T
            total = decay[length - 1 : length, :]
            scaled_k = (jnp.exp(total - decay) * k_ref[:, cols].astype(F32)).astype(BF16)
            scaled_q = (jnp.exp(decay) * q_ref[:, cols].astype(F32)).astype(BF16)
            state = dot(scaled_k, v_ref[:, cols], 0, 0).astype(BF16)
            adjoint = dot(scaled_q, c_ref[:, cols], 0, 0).astype(BF16)
            gains = split_rows(jnp.exp(total))
            for part in range(4):
                rows = slice(part * chunk, (part + 1) * chunk)
                left = slice((4 * i + part) * size, (4 * i + part + 1) * size)
                right = slice(width + (4 * i + part) * size, width + (4 * i + part + 1) * size)
                outs[m][0:chunk, left] = state[rows]
                outs[m][0:chunk, right] = adjoint[rows]
                outs[m][chunk:STATE_ROWS, left] = gains
                outs[m][chunk:STATE_ROWS, right] = gains


def plane_kernel(p_ref, x0, x1, x2, x3, out_ref):
    spots = [p_ref[0] ^ m for m in range(INNER)]
    xs = (x0, x1, x2, x3)
    width = out_ref.shape[1] // 2
    rows = STATE_ROWS - PAD
    gains = [join_rows(x[rows:STATE_ROWS, 0:width]) for x in xs]
    ones = jnp.ones_like(gains[0])
    up = jnp.zeros((rows, width), F32)
    down = jnp.zeros((rows, width), F32)
    for m in range(INNER):
        behind, before = ones, ones
        for j in range(INNER):
            behind = behind * jnp.where(spots[j] > spots[m], gains[j], ones)
            before = before * jnp.where(spots[j] < spots[m], gains[j], ones)
        up = up + behind * xs[m][0:rows, 0:width].astype(F32)
        down = down + before * xs[m][0:rows, width:].astype(F32)
    total = split_rows(gains[0] * gains[1] * gains[2] * gains[3])
    out_ref[0:rows, 0:width] = up.astype(BF16)
    out_ref[0:rows, width:] = down.astype(BF16)
    out_ref[rows:, 0:width] = total
    out_ref[rows:, width:] = total


def scan_planes(plane, own, others):
    width = own.shape[1] // 2
    rows = STATE_ROWS - PAD
    gain = join_rows(own[rows:, 0:width])
    ones = jnp.ones_like(gain)
    up = own[0:rows, 0:width].astype(F32)
    down = own[0:rows, width:].astype(F32)
    below = jnp.zeros_like(up)
    above = jnp.zeros_like(down)
    gain_below, gain_above = ones, ones
    for number, ref in enumerate(others):
        high = (plane & (1 << number)) != 0
        their_up = ref[0:rows, 0:width].astype(F32)
        their_down = ref[0:rows, width:].astype(F32)
        their_gain = join_rows(ref[rows:, 0:width])
        below = jnp.where(high, below + gain_below * their_up, below)
        gain_below = jnp.where(high, gain_below * their_gain, gain_below)
        above = jnp.where(high, above, above + gain_above * their_down)
        gain_above = jnp.where(high, gain_above, gain_above * their_gain)
        up = jnp.where(high, up + gain * their_up, their_up + their_gain * up)
        down = jnp.where(high, their_down + their_gain * down, down + gain * their_down)
        gain = gain * their_gain
    return up, down, gain, below, gain_below, above, gain_above


def join_kernel(last, p_ref, own, *refs):
    out_ref = refs[-1]
    plane = p_ref[1]
    rows = STATE_ROWS - PAD
    up, down, gain, *_ = scan_planes(plane, own, refs[:-1])
    if last:
        high = (plane & (1 << (len(refs) - 1))) != 0
        out_ref[0:rows, :] = jnp.where(high, down, up).astype(BF16)
        out_ref[rows:, :] = split_rows(gain)
        return
    width = up.shape[1]
    out_ref[0:rows, 0:width] = up.astype(BF16)
    out_ref[0:rows, width:] = down.astype(BF16)
    out_ref[rows:, 0:width] = split_rows(gain)
    out_ref[rows:, width:] = split_rows(gain)


def spread_kernel(p_ref, x0, x1, x2, x3, own, *refs):
    spots = [p_ref[0] ^ m for m in range(INNER)]
    plane = p_ref[1]
    xs, outs = (x0, x1, x2, x3), refs[-INNER:]
    others, final = refs[: -INNER - 1], refs[-INNER - 1]
    width = own.shape[1] // 2
    rows = STATE_ROWS - PAD
    gains = [join_rows(x[rows:STATE_ROWS, 0:width]) for x in xs]
    ones = jnp.ones_like(gains[0])
    zeros = jnp.zeros_like(gains[0])
    _, _, _, below, gain_below, above, gain_above = scan_planes(plane, own, others)
    high = (plane & (1 << len(others))) != 0
    far = final[0:rows, :].astype(F32)
    below = jnp.where(high, below + gain_below * far, below)
    above = jnp.where(high, above, above + gain_above * far)
    keys = [x[0:rows, 0:width].astype(F32) for x in xs]
    queries = [x[0:rows, width:].astype(F32) for x in xs]
    for m in range(INNER):
        first, last = ones, ones
        for j in range(INNER):
            first = first * jnp.where(spots[j] < spots[m], gains[j], ones)
            last = last * jnp.where(spots[j] > spots[m], gains[j], ones)
        state = first * below
        adjoint = last * above
        for i in range(INNER):
            if i == m:
                continue
            between = ones
            for j in range(INNER):
                if j == m or j == i:
                    continue
                inside = ((spots[j] > spots[i]) & (spots[j] < spots[m])) | (
                    (spots[j] < spots[i]) & (spots[j] > spots[m])
                )
                between = between * jnp.where(inside, gains[j], ones)
            state = state + jnp.where(spots[i] < spots[m], between, zeros) * keys[i]
            adjoint = adjoint + jnp.where(spots[i] > spots[m], between, zeros) * queries[i]
        outs[m][0:rows, :] = state.astype(BF16)
        outs[m][rows:, :] = adjoint.astype(BF16)


def decays(b_ref, head, length):
    across_rows = jnp.broadcast_to(b_ref[pl.ds(head, 1), :], (length, length))
    decay = across_rows.T
    return across_rows, decay, decay[length - 1 : length, :]


def inner_kernel(q_ref, k_ref, v_ref, c_ref, b_ref, dq_ref, dk_ref, dv_ref, flag_ref):
    flag_ref[...] = jnp.zeros_like(flag_ref)
    heads, length = b_ref.shape
    size = q_ref.shape[1] // heads
    row = lax.broadcasted_iota(jnp.int32, (length, length), 0)
    col = lax.broadcasted_iota(jnp.int32, (length, length), 1)
    causal = row >= col
    for head in range(heads):
        cols = slice(head * size, (head + 1) * size)
        across_rows, decay, _ = decays(b_ref, head, length)
        mask = jnp.where(causal, jnp.exp(jnp.where(causal, decay - across_rows, 0.0)), 0.0)
        q, k, v, c = q_ref[:, cols], k_ref[:, cols], v_ref[:, cols], c_ref[:, cols]
        w = (dot(c, v, 1, 1) * mask).astype(BF16)
        z = (dot(q, k, 1, 1) * mask).astype(BF16)
        dq_ref[:, cols] = dot(w, k, 1, 0)
        dk_ref[:, cols] = dot(w, q, 0, 0)
        dv_ref[:, cols] = dot(z, c, 0, 0)


def outer_kernel(p_ref, k_ref, v_ref, c_ref, b_ref, eq_ref, ek_ref, ev_ref, s0, s1, s2, s3, *outs):
    place = p_ref[0]
    states = (s0, s1, s2, s3)
    dq_ref, dk_ref, dv_ref, flag_ref = outs
    flag_ref[...] = jnp.zeros_like(flag_ref)
    heads, length = b_ref.shape
    size = k_ref.shape[1] // heads
    share = heads // INNER
    chunk = size // 4
    scale = 1.0 / size
    for m in range(INNER):
        quarter = place ^ m
        for i in range(share):
            head = quarter * share + i
            cols = pl.ds(pl.multiple_of(head * size, size), size)
            _, decay, total = decays(b_ref, head, length)
            lead = jnp.exp(decay)
            tail = jnp.exp(total - decay)
            k, v, c = k_ref[:, cols], v_ref[:, cols], c_ref[:, cols]
            tiles = [slice((4 * i + part) * size, (4 * i + part + 1) * size) for part in range(4)]
            state = jnp.concatenate([states[m][0:chunk, t] for t in tiles], axis=0)
            adjoint = jnp.concatenate([states[m][chunk : 2 * chunk, t] for t in tiles], axis=0)
            dq = eq_ref[:, cols] + lead * dot(c, state, 1, 1)
            dk = ek_ref[:, cols] + tail * dot(v, adjoint, 1, 1)
            dv = ev_ref[:, cols] + tail * dot(k, adjoint, 1, 0)
            dq_ref[:, cols] = (dq * scale).astype(BF16)
            dk_ref[:, cols] = (dk * scale).astype(BF16)
            dv_ref[:, cols] = (dv * scale).astype(BF16)


def pack_kernel(x_hbm, c_hbm, ids_hbm, gates_hbm, out_hbm, ids_ref, gates_ref, meta_ref, sems):
    tokens, width = x_hbm.shape
    top = ids_hbm.shape[0]
    pairs = [
        (ids_hbm, ids_ref),
        (gates_hbm, gates_ref),
        (x_hbm, out_hbm.at[:, 0:width]),
        (c_hbm, out_hbm.at[:, width : 2 * width]),
    ]
    copies = [pltpu.make_async_copy(a, b, sems.at[i]) for i, (a, b) in enumerate(pairs)]
    for copy in copies:
        copy.start()
    copies[0].wait()
    copies[1].wait()
    lists = [ids_ref[...].astype(F32), gates_ref[...].astype(F32)]
    lists.append(jnp.zeros((META - 2 * top, tokens), F32))
    meta_ref[...] = jnp.concatenate(lists, axis=0).T.astype(BF16)
    rest = pltpu.make_async_copy(meta_ref, out_hbm.at[:, 2 * width :], sems.at[4])
    rest.start()
    copies[2].wait()
    copies[3].wait()
    rest.wait()


def dispatch(block_ref, place, plane, cap, top):
    tokens, columns = block_ref.shape
    width = columns - META
    meta = block_ref[:, width:].astype(F32)
    j = lax.broadcasted_iota(jnp.int32, (tokens, INNER * cap), 1)
    part = jnp.zeros_like(j)
    for m in range(1, INNER):
        part = part + (j >= m * cap).astype(jnp.int32)
    expert = plane * INNER + (place ^ part)
    slots = (j - part * cap).astype(F32)
    expert = expert.astype(F32)
    named = jnp.zeros((tokens, INNER * cap), F32)
    weight = named
    for t in range(top):
        same = meta[:, t : t + 1] == expert
        named = jnp.where(same, 1.0, named)
        weight = jnp.where(same, meta[:, top + t : top + t + 1], weight)
    row = lax.broadcasted_iota(jnp.int32, (tokens, tokens), 0)
    col = lax.broadcasted_iota(jnp.int32, (tokens, tokens), 1)
    earlier = jnp.where(row > col, 1.0, 0.0).astype(BF16)
    rank = dot(earlier, named.astype(BF16), 1, 0)
    here = jnp.where(rank == slots, named, 0.0)
    weight = here * weight
    here = here.astype(BF16)
    rows = dot(here, block_ref[:, 0:width], 0, 0).astype(BF16)
    return rows, here, weight.astype(BF16)


def combine_kernel(base, carries, last, *refs):
    here_ref, weight_ref = refs[0:2]
    parts = refs[2 : 2 + INNER]
    cap = here_ref.shape[1] // INNER
    width = parts[0].shape[1] - META
    rows = jnp.concatenate([x[base : base + cap, :] for x in parts], axis=0)
    grads = dot(weight_ref[...], rows[:, 0:width], 1, 0)
    gates = dot(here_ref[...], rows[:, width:], 1, 0)
    for carry in refs[2 + INNER : 2 + INNER + carries]:
        grads = grads + carry[:, 0:width].astype(F32)
        gates = gates + carry[:, width:].astype(F32)
    if not last:
        refs[-1][:, 0:width] = grads.astype(BF16)
        refs[-1][:, width:] = gates.astype(BF16)
        return
    ids_ref, grad_ref, gate_ref = refs[-3:]
    grad_ref[...] = grads.astype(BF16)
    top, tokens = ids_ref.shape
    gates = gates.T
    row = lax.broadcasted_iota(jnp.int32, (META, tokens), 0)
    for t in range(top):
        mine = ids_ref[t : t + 1, :] == row
        picked = jnp.sum(jnp.where(mine, gates, 0.0), axis=0, keepdims=True)
        gate_ref[t : t + 1, :] = picked.astype(BF16)


def front_kernel(count, cap, *refs):
    parts, (up_ref, down_ref, pre_ref, back_ref) = refs[:-4], refs[-4:]
    width = up_ref.shape[1]
    rows = jnp.concatenate([x[x.shape[0] - cap :, :] for x in parts], axis=0)
    pre_ref[...] = dot(rows[:, 0:width], up_ref[0], 1, 0).astype(BF16)
    back_ref[...] = dot(rows[:, width:], down_ref[0], 1, 1).astype(BF16)


def back_kernel(slots, cap, i_ref, *refs):
    sums, up_ref, outs = refs[: -INNER - 1], refs[-INNER - 1], refs[-INNER:]
    width = up_ref.shape[1]
    half = len(sums) // 2
    totals = []
    for refs in (sums[:half], sums[half:]):
        terms = [ref[i].astype(F32) for ref in refs for i in range(ref.shape[0])]
        total = terms[0]
        for term in terms[1:]:
            total = total + term
        totals.append(total)
    pre, back = totals
    sig = 1.0 / (1.0 + jnp.exp(-pre))
    gate_back = jnp.sum(back * pre * sig, axis=1, keepdims=True)
    slope = (back * (sig * (1.0 + pre * (1.0 - sig)))).astype(BF16)
    lane = lax.broadcasted_iota(jnp.int32, (slope.shape[0], META), 1)
    gates = jnp.where(lane == i_ref[0], gate_back, 0.0).astype(BF16)
    grads = dot(slope, up_ref[0], 1, 1).astype(BF16)
    for s in range(slots):
        for m in range(INNER):
            source = slice((s * INNER + m) * cap, (s * INNER + m + 1) * cap)
            target = slice(s * cap, (s + 1) * cap)
            outs[m][target, 0:width] = grads[source]
            outs[m][target, width:] = gates[source]


def body(q, k, v, log_decay, cot, expert_input, router_gates, expert_ids, up_weights, down_weights):
    n = lax.axis_size("ctx")
    planes = n // INNER
    index = lax.axis_index("ctx").astype(jnp.int32)
    spots = jnp.stack([index % INNER, index // INNER])
    where = index.reshape(1)
    tokens, width = expert_input.shape
    top = expert_ids.shape[1]
    cap = 5 * tokens * top // (4 * n)
    heads = log_decay.shape[0]
    size = width // heads
    hidden = up_weights.shape[2]
    ids, gates = expert_ids.T, router_gates.T

    (block,) = call(
        pack_kernel,
        "pack",
        [((tokens, 2 * width + META), BF16)],
        [IN_HBM] * 4,
        *[pltpu.with_memory_space_constraint(x, pltpu.HBM) for x in (expert_input, cot, ids, gates)],
        scratch=[
            pltpu.VMEM((top, tokens), expert_ids.dtype),
            pltpu.VMEM((top, tokens), BF16),
            pltpu.VMEM((tokens, META), BF16),
            pltpu.SemaphoreType.DMA((5,)),
        ],
        where=IN_HBM,
    )
    blocks = [block]
    for _ in range(planes - 1):
        blocks.append(ring(blocks[-1]))

    row = lax.broadcasted_iota(jnp.int32, (tokens, tokens), 0)
    col = lax.broadcasted_iota(jnp.int32, (tokens, tokens), 1)
    cumul = jnp.dot(log_decay, (row <= col).astype(F32), precision=lax.Precision.HIGHEST)
    table = ((tokens, INNER * cap), BF16)
    sent, tables, answers, carry, direct = {}, {}, {}, [], []

    def dispatch_into(start, p_ref, x_ref, outs):
        rows, here, weight = dispatch(x_ref, p_ref[0], p_ref[1], cap, top)
        for m in range(INNER):
            outs[m][start:, :] = rows[m * cap : (m + 1) * cap]
        outs[INNER][...] = here
        outs[INNER + 1][...] = weight

    def first_kernel(p_ref, x_ref, q_ref, k_ref, v_ref, c_ref, b_ref, *outs):
        states_into(p_ref[0], q_ref, k_ref, v_ref, c_ref, b_ref, outs)
        dispatch_into(STATE_ROWS, p_ref, x_ref, outs)

    def next_kernel(p_ref, x_ref, *outs):
        dispatch_into(0, p_ref, x_ref, outs)

    def serve(r, previous):
        if r == 0:
            outs = call(
                first_kernel,
                "first_slot",
                [((STATE_ROWS + cap, 2 * width), BF16)] * INNER + [table] * 2,
                [IN_SMEM] + [IN_VMEM] * 6,
                spots,
                block,
                q,
                k,
                v,
                cot,
                cumul,
            )
        else:
            outs = call(
                next_kernel,
                "next_slot",
                [((cap, 2 * width), BF16)] * INNER + [table] * 2,
                [IN_SMEM, IN_VMEM],
                spots,
                blocks[r],
                needs=[previous],
            )
        sent[r] = exchange(outs[:INNER])
        tables[r] = outs[INNER:]
        return tables[r][0]

    def front(group, *needs):
        parts = [x for r in group for x in sent[r]]

        def kernel(*refs):
            front_kernel(len(group), cap, *refs)

        own = call(
            kernel,
            "expert_front",
            [((len(parts) * cap, hidden), BF16)] * 2,
            [IN_VMEM] * (len(parts) + 2),
            *parts,
            up_weights,
            down_weights,
            needs=needs,
        )
        if lax.axis_size("exp") == 2 and len(group) > 1:
            other = [lax.ppermute(x, "exp", [(0, 1), (1, 0)]) for x in own]
            return own[0], [own[0][None], other[0][None], own[1][None], other[1][None]]
        return own[0], [lax.all_gather(x, "exp") for x in own]

    def finish(group, sums, *needs):
        def kernel(*refs):
            back_kernel(len(group), cap, *refs)

        outs = call(
            kernel,
            "expert_back",
            [((len(group) * cap, width + META), BF16)] * INNER,
            [IN_SMEM] + [IN_VMEM] * (len(sums) + 1),
            where,
            *sums,
            up_weights,
            needs=needs,
        )
        got = exchange(outs)
        for s, r in enumerate(group):
            answers[r] = (s * cap, got)
        return outs[0]

    def combine(r, *needs):
        base, got = answers[r]
        last = r == 0

        if last:
            carry.extend(direct)

        def kernel(*refs, carried=len(carry)):
            combine_kernel(base, carried, last, *refs)

        extra = carry + ([ids] if last else [])
        whole = ((tokens, width), BF16), ((top, tokens), BF16)
        outs = call(
            kernel,
            "combine",
            whole if last else [((tokens, width + META), BF16)],
            [IN_VMEM] * (2 + INNER + len(extra)),
            *tables[r],
            *got,
            *extra,
            needs=needs,
        )
        if r == 1:
            direct.append(unring(outs[0]))
        elif not last:
            carry[:] = [ring(outs[0])]
        return outs

    def plane_sums(previous):
        (total,) = call(
            plane_kernel,
            "plane_sums",
            [((STATE_ROWS, 2 * width), BF16)],
            [IN_SMEM] + [IN_VMEM] * INNER,
            spots,
            *sent[0],
            needs=[previous],
        )
        others.append(plane_flip(total, 1))
        return total

    def join(step, previous):
        last = 2 * step >= planes

        def kernel(*refs):
            join_kernel(last, *refs)

        (joined,) = call(
            kernel,
            "join_planes",
            [((STATE_ROWS, width if last else 2 * width), BF16)],
            [IN_SMEM] + [IN_VMEM] * (1 + len(others)),
            spots,
            plane_sum,
            *others,
            needs=[previous],
        )
        others.append(plane_flip(joined, step))
        return joined

    others = []
    previous = serve(0, None)
    early = call(
        inner_kernel,
        "inner_grads",
        [(q.shape, F32)] * 3 + [((8, 128), F32)],
        [IN_VMEM] * 5,
        q,
        k,
        v,
        cot,
        cumul,
        needs=[previous],
    )
    previous = serve(1, early[3])
    previous, sums = front([0, 1], previous)
    previous = serve(2, previous)
    previous = finish([0, 1], sums, previous)
    previous = plane_sum = plane_sums(previous)
    previous, sums = front([2], previous)
    for r in range(3, planes):
        previous = finish([r - 1], sums, previous)
        previous = combine(r - 2, previous, others[0])[0]
        previous = serve(r, previous)
        if r == 3:
            step = 2
            while step < planes:
                previous = join(step, previous)
                step *= 2
        previous, sums = front([r], previous, *direct)
        if r == planes - 1:
            previous = combine(planes - 2, previous)[0]
    previous = finish([planes - 1], sums, previous, others[-1])
    states = call(
        spread_kernel,
        "spread_states",
        [((size // 2, width), BF16)] * INNER,
        [IN_SMEM] + [IN_VMEM] * (INNER + 1 + len(others)),
        spots,
        *sent[0],
        plane_sum,
        *others,
        needs=[previous],
    )
    previous = combine(planes - 1, states[0])[0]
    states = exchange(states)
    grads = call(
        outer_kernel,
        "outer_grads",
        [(q.shape, BF16)] * 3 + [((8, 128), F32)],
        [IN_SMEM] + [IN_VMEM] * (7 + INNER),
        spots,
        k,
        v,
        cot,
        cumul,
        *early[:3],
        *states,
        needs=[previous],
    )
    input_grad, gate_grad = combine(0, grads[3])
    return (*grads[:3], input_grad, gate_grad.T)


def solution(mesh):
    rows = P("ctx", "exp")
    return jax.shard_map(
        body,
        mesh=mesh,
        in_specs=(
            rows,
            rows,
            rows,
            P("exp", "ctx"),
            rows,
            rows,
            P("ctx", None),
            P("ctx", None),
            P("ctx", "exp", None),
            P("ctx", None, "exp"),
        ),
        out_specs=(rows, rows, rows, rows, P("ctx", None)),
        check_vma=False,
    )
```
